128 devices in a mesh: group: 2 (over x_lo), tile: 64 (over z, x_hi, y, core).
Axes of the slice: x: 4 (x_hi: 2, x_lo: 2; x = x_hi * 2 + x_lo), y: 4, z: 4, core: 2. Of those that a mesh axis runs over, the one named last changes fastest.
Arguments:
- east_wind: float32 [2, 8, 1024, 2048], P('group', None, 'tile'), may hold values from -6 to 6
- equator_wind: float32 [2, 8, 1024, 2048], P('group', None, 'tile'), may hold values from -6 to 6
- pressure: float32 [2, 8, 1024, 2048], P('group', None, 'tile'), may hold values from -6 to 6
- moisture: float32 [2, 8, 1024, 2048], P('group', None, 'tile'), may hold values from 0.05 to 0.5
- albedo: float32 [2, 1024, 2048], P('group', 'tile'), may hold values from 0.05 to 0.8
- courant: float32 [8], replicated, may hold values from 0.3 to 1.2
- sun_angles: float32 [2], replicated, may hold values from -3.140625 to 3.140625
- absorption: float32 [256], replicated, may hold values from 0.01 to 30
- solar_weights: float32 [256], replicated, may hold values from 0.05 to 5
Outputs:
- east_wind_next: float32 [2, 8, 1024, 2048], P('group', None, 'tile')
- equator_wind_next: float32 [2, 8, 1024, 2048], P('group', None, 'tile')
- pressure_next: float32 [2, 8, 1024, 2048], P('group', None, 'tile')
The draws below stay inside these ranges and needn't reach their ends.
All inputs are finite; a program needn't handle non-finite values.
Results may differ from the reference program's by a relative error of at most 0.0001.
Values sent between devices are 32-bit elements; how exact they have to be, the bound alone decides.
No kernel may reach another device: no remote copies, remote signals or barrier semaphores. Data moves between devices by JAX's collectives and lax.ppermute only.
A program may use at most 128 MiB of HBM per device.

```python
import math
import jax
import jax.numpy as jnp
from jax import lax

LEV = 8
G = 256
SUB = 6
NYH = 1024
NX = 2048


def levels(key, dims, pieces, smallest, high):
    gain, own = 1.0, jax.random.fold_in(key, 6)
    for axis_at, shards_of in pieces:
        heights = jnp.exp(jax.random.uniform(jax.random.fold_in(own, axis_at), (shards_of,), jnp.float32, smallest / len(pieces), high / len(pieces)))
        gain = gain * jnp.repeat(heights, dims[axis_at] // shards_of).reshape([-1 if axis == axis_at else 1 for axis in range(len(dims))])
    return gain


def normal_values(key, dims, width, reach, pieces=(), kind=jnp.bfloat16):
    gain = levels(key, dims, pieces, -0.22, 0.18) if pieces else 1.0
    result = jax.random.normal(key, dims, jnp.float32) * width * gain
    return jnp.minimum(jnp.maximum(result, -reach), reach).astype(kind)


def setup_inputs(seed: int = 0) -> dict:
    splits = jax.random.split(jax.random.key(seed), 10)
    return {
        "east_wind": normal_values(splits[0], (2, LEV, NYH, NX), 1.0, 6.0, ((0, 2), (2, 64)), jnp.float32),
        "equator_wind": normal_values(splits[1], (2, LEV, NYH, NX), 1.0, 6.0, ((0, 2), (2, 64)), jnp.float32),
        "pressure": normal_values(splits[2], (2, LEV, NYH, NX), 1.0, 6.0, ((0, 2), (2, 64)), jnp.float32),
        "moisture": jnp.clip(0.05 + 0.45 * jax.random.uniform(splits[3], (2, LEV, NYH, NX), jnp.float32) ** levels(splits[3], (2, LEV, NYH, NX), ((0, 2), (2, 64)), -0.2, 0.2), 0.05, 0.5),
        "albedo": jnp.clip(0.05 + 0.75 * jax.random.uniform(splits[4], (2, NYH, NX), jnp.float32) ** levels(splits[4], (2, NYH, NX), ((0, 2), (1, 64)), -0.2, 0.2), 0.05, 0.8),
        "courant": jnp.clip(jnp.exp(jax.random.uniform(splits[5], (LEV,), jnp.float32, math.log(0.3), math.log(1.2))), 0.3, 1.2),
        "sun_angles": jnp.clip(jax.random.uniform(splits[6], (2,), jnp.float32, -3.140625, 3.140625), -3.140625, 3.140625),
        "absorption": jnp.clip(jnp.exp(jax.random.uniform(splits[7], (G,), jnp.float32, math.log(0.01), math.log(30.0))), 0.01, 30.0),
        "solar_weights": jnp.clip(jnp.exp(jax.random.uniform(splits[8], (G,), jnp.float32, math.log(0.05), math.log(5.0))), 0.05, 5.0),
    }


HEAT_SCALE = 10.0
MU_OFFSET = 0.1
DIFFUSE = 1.66


def centred_rows(values, mirror_sign):
    pole_rim = jnp.zeros_like(values[:, :, :1, :])
    equator = mirror_sign * values[::-1, :, -1:, :]
    extended = jnp.concatenate([pole_rim, values, equator], axis=2)
    return extended[:, :, 2:, :], extended[:, :, :-2, :]


def radiate(absorber, sun_cos, surface, absorption, solar_weights):
    sunlit = jnp.maximum(sun_cos, 0.0)
    slant_path = 1.0 / (sunlit + MU_OFFSET)
    optical_depth = jnp.concatenate([jnp.zeros_like(absorber[:1]), jnp.cumsum(absorber, axis=0)], axis=0)
    column_depth = optical_depth[-1:]
    coeffs = absorption.reshape((-1,) + (1,) * optical_depth.ndim)
    down_flux = jnp.exp(-coeffs * (optical_depth * slant_path))
    up_flux = jnp.exp(-coeffs * (column_depth * slant_path + DIFFUSE * (column_depth - optical_depth)))
    weights = (solar_weights / solar_weights.shape[0]).reshape(coeffs.shape)
    net_flux = jnp.sum(weights * (down_flux - surface * up_flux), axis=0) * sunlit
    return HEAT_SCALE * (net_flux[:-1] - net_flux[1:])


def sun_cosine(latitude, longitude, sun_angles):
    declination = 0.41 * jnp.sin(sun_angles[0])
    return (jnp.sin(latitude)[:, None] * jnp.sin(declination)
            + jnp.cos(latitude)[:, None] * jnp.cos(declination) * jnp.cos(longitude[None, :] - sun_angles[1]))


def reference(east_wind, equator_wind, pressure, moisture, albedo, courant, sun_angles, absorption, solar_weights):
    courant_col = courant[None, :, None, None]
    for substep in range(SUB):
        ahead_wind, behind_wind = centred_rows(equator_wind, -1.0)
        divergence = 0.5 * (jnp.roll(east_wind, -1, 3) - jnp.roll(east_wind, 1, 3) + ahead_wind - behind_wind)
        pressure = pressure - courant_col * divergence
        ahead_press, behind_press = centred_rows(pressure, 1.0)
        east_wind = east_wind - courant_col * (0.5 * (jnp.roll(pressure, -1, 3) - jnp.roll(pressure, 1, 3)))
        equator_wind = equator_wind - courant_col * (0.5 * (ahead_press - behind_press))
    half_rows = NYH // 2
    half_cols = NX // 2
    coarse_moist = moisture.reshape(2, LEV, half_rows, 2, half_cols, 2).mean(axis=(3, 5))
    coarse_albedo = albedo.reshape(2, half_rows, 2, half_cols, 2).mean(axis=(2, 4))
    colatitude = 1.0 - (jnp.arange(half_rows).astype(jnp.float32) + 0.5) / half_rows
    longitude = 2.0 * jnp.pi * (jnp.arange(half_cols).astype(jnp.float32) + 0.5) / half_cols

    def one_row(packed):
        absorber_row, sun_row, surface_row = packed
        return radiate(absorber_row, sun_row, surface_row, absorption, solar_weights)

    heat_parts = []
    for hemisphere in range(2):
        sign_value = 2.0 * hemisphere - 1.0
        latitude = sign_value * (0.5 * jnp.pi) * colatitude
        sun_cos = sun_cosine(latitude, longitude, sun_angles)
        absorber_rows = jnp.moveaxis(coarse_moist[hemisphere], 1, 0)
        heat_rows = lax.map(one_row, (absorber_rows, sun_cos, coarse_albedo[hemisphere]))
        heat_parts.append(jnp.moveaxis(heat_rows, 0, 1))
    heating = jnp.stack(heat_parts)
    fine_heat = jnp.repeat(jnp.repeat(heating, 2, axis=2), 2, axis=3)
    return east_wind, equator_wind, pressure + fine_heat
```

```python
import functools
import math

import jax
import jax.numpy as jnp
from jax import lax
from jax.experimental import pallas as pl
from jax.experimental.pallas import tpu as pltpu
from jax.sharding import PartitionSpec as P

SUB = 6
HEAT_SCALE = 10.0
MU_OFFSET = 0.1
DIFFUSE = 1.66
LOG2E = 1.4426950408889634
LANES = 128
OFF = 8

VMEM = pltpu.VMEM
SMEM = pltpu.SMEM
F32 = jnp.float32


def lane_iota(dtype=jnp.int32):
    return lax.broadcasted_iota(dtype, (8, LANES), 1)


def sub_iota():
    return lax.broadcasted_iota(jnp.int32, (8, LANES), 0)


def coarsen_kernel(moist, albedo, keep, send):
    width = moist.shape[-1]
    half = keep.shape[-1] // LANES
    even_row = sub_iota() % 2 == 0
    even_lane = lane_iota() % 2 == 0

    def fold(top, bottom):
        return jnp.where(
            even_row, top + pltpu.roll(top, 7, 0), bottom + pltpu.roll(bottom, 1, 0)
        )

    def pack(left, right):
        return jnp.where(
            even_lane,
            left + pltpu.roll(left, LANES - 1, 1),
            right + pltpu.roll(right, 1, 1),
        )

    for level in range(9):
        for block in range(width // (2 * LANES)):
            parts = []
            for side in range(2):
                cols = pl.ds((2 * block + side) * LANES, LANES)
                if level < 8:
                    parts.append((moist[level, 0:8, cols], moist[level, 8:16, cols]))
                else:
                    parts.append((albedo[0:8, cols], albedo[8:16, cols]))
            top = pack(parts[0][0], parts[1][0])
            bottom = pack(parts[0][1], parts[1][1])
            value = fold(top, bottom) * 0.25
            if block < half:
                keep[level, :, pl.ds(block * LANES, LANES)] = value
            else:
                send[level, :, pl.ds((block - half) * LANES, LANES)] = value


def radiate_kernel(
    rows_total, cols_total, sun, absorption, weights, own, other, heat_own, heat_other
):
    group = lax.axis_index("group")
    tile = lax.axis_index("tile")
    sublane = sub_iota()
    lane = lane_iota()
    row = tile * 8 + sublane // 2 + 4 * (sublane % 2)
    colatitude = 1.0 - (row.astype(F32) + 0.5) / rows_total
    hemisphere = 2.0 * group.astype(F32) - 1.0
    latitude = hemisphere * (0.5 * math.pi) * colatitude
    declination = 0.41 * jnp.sin(jnp.full((8, LANES), sun[0], F32))
    sine = jnp.sin(latitude) * jnp.sin(declination)
    cosine = jnp.cos(latitude) * jnp.cos(declination)
    n_g = absorption.shape[0]

    for block in range(own.shape[-1] // LANES):
        cols = pl.ds(block * LANES, LANES)
        column = block * LANES + lane // 2 + 64 * (lane % 2)
        longitude = 2.0 * math.pi * (column.astype(F32) + 0.5) / cols_total
        mu = sine + cosine * jnp.cos(longitude - sun[1])
        lit = mu > 0.0
        sunlit = jnp.abs(mu)
        slant = 1.0 / (sunlit + MU_OFFSET)
        depth = [jnp.zeros((8, LANES), F32)]
        for level in range(8):
            layer = jnp.where(lit, own[level, :, cols], other[level, :, cols])
            depth.append(depth[-1] + layer)
        surface = jnp.where(lit, own[8, :, cols], other[8, :, cols])
        total = depth[8]
        direct = total * slant
        paths = [depth[j] * slant for j in range(1, 9)]
        paths += [direct + DIFFUSE * (total - depth[j]) for j in range(8)]

        def body(g, carry):
            rate = absorption[g] * (-LOG2E)
            weight = weights[g]
            sums, whole = carry[:-1], carry[-1]
            sums = tuple(a + weight * jnp.exp2(rate * p) for a, p in zip(sums, paths))
            return sums + (whole + weight,)

        zero = jnp.zeros((8, LANES), F32)
        sums = lax.fori_loop(0, n_g, body, (zero,) * 17, unroll=32)
        down = (sums[16],) + sums[:8]
        up = sums[8:16] + (sums[7],)
        scale = sunlit * (HEAT_SCALE / n_g)
        net = [scale * (down[j] - surface * up[j]) for j in range(9)]
        for level in range(8):
            heat = net[level] - net[level + 1]
            heat_own[level, :, cols] = jnp.where(lit, heat, 0.0)
            heat_other[level, :, cols] = jnp.where(lit, 0.0, heat)


def courant_half(courant):
    level = sub_iota()
    value = jnp.full((8, LANES), courant[7], F32)
    for index in range(7):
        value = jnp.where(level == index, courant[index], value)
    return 0.5 * value


def load_row(ref, row):
    return [ref[row, :, pl.ds(j * LANES, LANES)] for j in range(ref.shape[-1] // LANES)]


def store_row(ref, row, values):
    for j, value in enumerate(values):
        ref[row, :, pl.ds(j * LANES, LANES)] = value


def shifted(values, by):
    count = len(values)
    turned = [pltpu.roll(v, (-by) % LANES, 1) for v in values]
    lane = lane_iota()
    if by > 0:
        edge = lane >= LANES - by
        return [jnp.where(edge, turned[(j + 1) % count], turned[j]) for j in range(count)]
    edge = lane < -by
    return [jnp.where(edge, turned[j - 1], turned[j]) for j in range(count)]


def stage(east_in, flow_in, press_in, east, flow, press, half):
    for block in range(2):
        rows = pl.ds(8 * block, 8)
        inner = pl.ds(OFF + 8 * block, 8)
        flow[inner] = jnp.swapaxes(flow_in[:, rows, :], 0, 1)
        east[inner] = jnp.swapaxes(east_in[:, rows, :], 0, 1)
        press[inner] = jnp.swapaxes(press_in[:, rows, :], 0, 1)
    for row in range(OFF, OFF + 16):
        store_row(east, row, shifted(load_row(east, row), 1))
        store_row(press, row, [half * v for v in load_row(press, row)])


def press_rows(rows, east, flow, press, rate):
    for row in rows:
        here = load_row(east, row)
        back = shifted(here, -2)
        ahead, behind = load_row(flow, row + 1), load_row(flow, row - 1)
        old = load_row(press, row)
        store_row(
            press,
            row,
            [
                p - rate * ((e - b) + (n - s))
                for p, e, b, n, s in zip(old, here, back, ahead, behind)
            ],
        )


def east_rows(rows, east, press):
    for row in rows:
        here = load_row(press, row)
        ahead = shifted(here, 2)
        old = load_row(east, row)
        store_row(east, row, [e - (a - p) for e, a, p in zip(old, ahead, here)])


def flow_rows(rows, flow, press):
    for row in rows:
        ahead, behind = load_row(press, row + 1), load_row(press, row - 1)
        old = load_row(flow, row)
        store_row(flow, row, [q - (n - s) for q, n, s in zip(old, ahead, behind)])


def spans(*pairs):
    return [OFF + row for low, high in pairs for row in range(low, high + 1)]


PRESS_SPANS = [
    spans((-1, 16)),
    spans((-3, 18)),
    spans((-5, 6), (9, 20)),
    spans((-5, 4), (11, 20)),
    spans((-3, 2), (13, 18)),
    spans((-1, 0), (15, 16)),
]
EAST_SPANS = [
    spans((-1, 16)),
    spans((-3, 6), (9, 18)),
    spans((-5, 4), (11, 20)),
    spans((-3, 2), (13, 18)),
    spans((-1, 0), (15, 16)),
]
FLOW_SPANS = [
    spans((-2, 17)),
    spans((-4, 19)),
    spans((-6, 5), (10, 21)),
    spans((-4, 3), (12, 19)),
    spans((-2, 1), (14, 17)),
]


def alone_kernel(
    courant, east_in, flow_in, press_in, low_out, high_out, up, down, east, flow, press
):
    group = lax.axis_index("group")
    half = courant_half(courant)
    rate = half * half
    zero = jnp.zeros((8, LANES), F32)
    count = east.shape[-1] // LANES
    for row in spans((-8, -1), (16, 23)):
        for ref in (east, flow, press):
            store_row(ref, row, [zero] * count)
    stage(east_in, flow_in, press_in, east, flow, press, half)

    def record(slot, ref):
        store_row(low_out, slot, load_row(ref, OFF - 1))
        store_row(high_out, slot, load_row(ref, OFF + 16))
        first, last = load_row(ref, OFF), load_row(ref, OFF + 15)

        @pl.when(group == 0)
        def _():
            store_row(up, slot, last)
            store_row(down, slot, first)

        @pl.when(group != 0)
        def _():
            store_row(up, slot, first)
            store_row(down, slot, last)

    for step in range(SUB):
        record(step, flow)
        press_rows(PRESS_SPANS[step], east, flow, press, rate)
        record(SUB + step, press)
        if step < SUB - 1:
            east_rows(EAST_SPANS[step], east, press)
            flow_rows(FLOW_SPANS[step], flow, press)


def joined_kernel(
    n_tiles,
    courant,
    east_in,
    flow_in,
    press_in,
    low_own,
    high_own,
    from_before,
    from_after,
    east_out,
    flow_out,
    press_out,
    east,
    flow,
    press,
):
    group = lax.axis_index("group")
    tile = lax.axis_index("tile")
    half = courant_half(courant)
    rate = half * half
    stage(east_in, flow_in, press_in, east, flow, press, half)
    inner = range(OFF, OFF + 16)
    south = group == 0
    keep_low = jnp.where(tile == 0, 0.0, 1.0)
    turn = jnp.where(tile == n_tiles - 1, -1.0, 1.0)

    def border(slot, ref, sign):
        before, after = load_row(from_before, slot), load_row(from_after, slot)
        own_low, own_high = load_row(low_own, slot), load_row(high_own, slot)
        low, high = [], []
        for b, a, l, h in zip(before, after, own_low, own_high):
            low.append(keep_low * l + jnp.where(south, b, a))
            high.append(h + sign * jnp.where(south, a, b))
        store_row(ref, OFF - 1, low)
        store_row(ref, OFF + 16, high)

    def substep(step, carry):
        border(step, flow, turn)
        press_rows(inner, east, flow, press, rate)
        border(SUB + step, press, 1.0)
        east_rows(inner, east, press)
        flow_rows(inner, flow, press)
        return carry

    lax.fori_loop(0, SUB, substep, 0)
    inverse = 1.0 / half
    for row in inner:
        store_row(east, row, shifted(load_row(east, row), -1))
        store_row(press_out, row - OFF, [inverse * v for v in load_row(press, row)])
    for block in range(2):
        rows = pl.ds(8 * block, 8)
        source = pl.ds(OFF + 8 * block, 8)
        east_out[:, rows, :] = jnp.swapaxes(east[source], 0, 1)
        flow_out[:, rows, :] = jnp.swapaxes(flow[source], 0, 1)


def spread_kernel(press, heat_own, heat_back, out, heat_rows, sums):
    even_lane = lane_iota() % 2 == 0
    for source, part in enumerate((heat_own, heat_back)):
        width = part.shape[-1]
        heat_rows[:, :, pl.ds(source * width, width)] = jnp.swapaxes(part[...], 0, 1)
    for sublane in range(8):
        coarse = sublane // 2 + 4 * (sublane % 2)
        for block, value in enumerate(load_row(heat_rows, sublane)):
            left = jnp.where(even_lane, value, pltpu.roll(value, 1, 1))
            right = jnp.where(even_lane, pltpu.roll(value, LANES - 1, 1), value)
            for side, heat in enumerate((left, right)):
                cols = pl.ds((2 * block + side) * LANES, LANES)
                for row in (2 * coarse, 2 * coarse + 1):
                    sums[row, :, cols] = press[row, :, cols] + heat
    for block in range(2):
        rows = pl.ds(8 * block, 8)
        out[:, rows, :] = jnp.swapaxes(sums[rows], 0, 1)


def call(kernel, name, outs, n_smem, n_vmem, scratch=()):
    return pl.pallas_call(
        kernel,
        name=name,
        out_shape=[jax.ShapeDtypeStruct(s, F32) for s in outs],
        in_specs=[pl.BlockSpec(memory_space=SMEM)] * n_smem
        + [pl.BlockSpec(memory_space=VMEM)] * n_vmem,
        out_specs=[pl.BlockSpec(memory_space=VMEM)] * len(outs),
        scratch_shapes=[VMEM(s, F32) for s in scratch],
        cost_estimate=pl.CostEstimate(
            flops=10**7, bytes_accessed=10**7, transcendentals=0
        ),
    )


def shards(
    east_wind, equator_wind, pressure, moisture, albedo, courant, sun_angles, absorption, solar_weights
):
    east, flow, press, moist = east_wind[0], equator_wind[0], pressure[0], moisture[0]
    levels, rows, cols = east.shape
    n_tiles = lax.axis_size("tile")
    half_cols = cols // 4
    last = 2 * n_tiles - 1
    line = [t for t in range(n_tiles)] + [2 * n_tiles - 1 - t for t in range(n_tiles)]
    upward = [(line[i], line[i + 1]) for i in range(last)]
    downward = [(line[i + 1], line[i]) for i in range(last)]
    swap = [(0, 1), (1, 0)]

    coarse = (9, 8, half_cols)
    keep, send = call(coarsen_kernel, "coarsen", [coarse, coarse], 0, 2)(moist, albedo[0])
    other = lax.ppermute(send, "group", swap)

    series = (2 * SUB, 8, cols)
    work = [(rows + 2 * OFF, 8, cols)] * 3
    low, high, up, down = call(alone_kernel, "alone", [series] * 4, 1, 3, work)(
        courant, east, flow, press
    )
    from_before = lax.ppermute(up, ("group", "tile"), upward)
    from_after = lax.ppermute(down, ("group", "tile"), downward)

    heat = (8, 8, half_cols)
    heat_own, heat_other = call(
        functools.partial(radiate_kernel, n_tiles * rows // 2, cols // 2),
        "radiate",
        [heat, heat],
        3,
        2,
    )(sun_angles, absorption, solar_weights, keep, other)
    heat_back = lax.ppermute(heat_other, "group", swap)

    field = (levels, rows, cols)
    east, flow, press = call(
        functools.partial(joined_kernel, n_tiles),
        "joined",
        [field, field, (rows, 8, cols)],
        1,
        7,
        work,
    )(courant, east, flow, press, low, high, from_before, from_after)
    (press,) = call(
        spread_kernel, "spread", [field], 0, 3, [(8, 8, cols // 2), (rows, 8, cols)]
    )(press, heat_own, heat_back)
    return east[None], flow[None], press[None]


def solution(mesh):
    field = P("group", None, "tile", None)
    return jax.shard_map(
        shards,
        mesh=mesh,
        in_specs=(field,) * 4 + (P("group", "tile", None),) + (P(),) * 4,
        out_specs=(field,) * 3,
        check_vma=False,
    )
```

```python
import functools
import math

import jax
import jax.numpy as jnp
from jax import lax
from jax.experimental import pallas as pl
from jax.experimental.pallas import tpu as pltpu
from jax.sharding import PartitionSpec as P


SUB = 6
HEAT_SCALE = 10.0
MU_OFFSET = 0.1
DIFFUSE = 1.66
LOG2E = 1.4426950408889634
LANES = 128
OFF = 8

VMEM = pltpu.VMEM
SMEM = pltpu.SMEM
F32 = jnp.float32


def lane_iota(dtype=jnp.int32):
    return lax.broadcasted_iota(dtype, (8, LANES), 1)


def sub_iota():
    return lax.broadcasted_iota(jnp.int32, (8, LANES), 0)


def coarsen_kernel(moist, albedo, keep, send):
    width = moist.shape[-1]
    half = keep.shape[-1] // LANES
    even_row = sub_iota() % 2 == 0
    even_lane = lane_iota() % 2 == 0

    def fold(top, bottom):
        return jnp.where(
            even_row, top + pltpu.roll(top, 7, 0), bottom + pltpu.roll(bottom, 1, 0)
        )

    def pack(left, right):
        return jnp.where(
            even_lane,
            left + pltpu.roll(left, LANES - 1, 1),
            right + pltpu.roll(right, 1, 1),
        )

    for level in range(9):
        for block in range(width // (2 * LANES)):
            parts = []
            for side in range(2):
                cols = pl.ds((2 * block + side) * LANES, LANES)
                if level < 8:
                    parts.append((moist[level, 0:8, cols], moist[level, 8:16, cols]))
                else:
                    parts.append((albedo[0:8, cols], albedo[8:16, cols]))
            top = pack(parts[0][0], parts[1][0])
            bottom = pack(parts[0][1], parts[1][1])
            value = fold(top, bottom) * 0.25
            if block < half:
                keep[level, :, pl.ds(block * LANES, LANES)] = value
            else:
                send[level, :, pl.ds((block - half) * LANES, LANES)] = value


def radiate_kernel(
    rows_total, cols_total, sun, absorption, weights, own, other, heat_own, heat_other
):
    group = lax.axis_index("group")
    tile = lax.axis_index("tile")
    sublane = sub_iota()
    lane = lane_iota()
    row = tile * 8 + sublane // 2 + 4 * (sublane % 2)
    colatitude = 1.0 - (row.astype(F32) + 0.5) / rows_total
    hemisphere = 2.0 * group.astype(F32) - 1.0
    latitude = hemisphere * (0.5 * math.pi) * colatitude
    declination = 0.41 * jnp.sin(jnp.full((8, LANES), sun[0], F32))
    sine = jnp.sin(latitude) * jnp.sin(declination)
    cosine = jnp.cos(latitude) * jnp.cos(declination)
    n_g = absorption.shape[0]

    for block in range(own.shape[-1] // LANES):
        cols = pl.ds(block * LANES, LANES)
        column = block * LANES + lane // 2 + 64 * (lane % 2)
        longitude = 2.0 * math.pi * (column.astype(F32) + 0.5) / cols_total
        mu = sine + cosine * jnp.cos(longitude - sun[1])
        lit = mu > 0.0
        sunlit = jnp.abs(mu)
        slant = 1.0 / (sunlit + MU_OFFSET)
        depth = [jnp.zeros((8, LANES), F32)]
        for level in range(8):
            layer = jnp.where(lit, own[level, :, cols], other[level, :, cols])
            depth.append(depth[-1] + layer)
        surface = jnp.where(lit, own[8, :, cols], other[8, :, cols])
        total = depth[8]
        direct = total * slant
        paths = [depth[j] * slant for j in range(1, 9)]
        paths += [direct + DIFFUSE * (total - depth[j]) for j in range(8)]

        def body(g, carry):
            rate = absorption[g] * (-LOG2E)
            weight = weights[g]
            sums, whole = carry[:-1], carry[-1]
            sums = tuple(a + weight * jnp.exp2(rate * p) for a, p in zip(sums, paths))
            return sums + (whole + weight,)

        zero = jnp.zeros((8, LANES), F32)
        sums = lax.fori_loop(0, n_g, body, (zero,) * 17, unroll=32)
        down = (sums[16],) + sums[:8]
        up = sums[8:16] + (sums[7],)
        scale = sunlit * (HEAT_SCALE / n_g)
        net = [scale * (down[j] - surface * up[j]) for j in range(9)]
        for level in range(8):
            heat = net[level] - net[level + 1]
            heat_own[level, :, cols] = jnp.where(lit, heat, 0.0)
            heat_other[level, :, cols] = jnp.where(lit, 0.0, heat)


def courant_half(courant):
    level = sub_iota()
    value = jnp.full((8, LANES), courant[7], F32)
    for index in range(7):
        value = jnp.where(level == index, courant[index], value)
    return 0.5 * value


def load_row(ref, row):
    return [ref[row, :, pl.ds(j * LANES, LANES)] for j in range(ref.shape[-1] // LANES)]


def store_row(ref, row, values):
    for j, value in enumerate(values):
        ref[row, :, pl.ds(j * LANES, LANES)] = value


def shifted(values, by):
    count = len(values)
    turned = [pltpu.roll(v, (-by) % LANES, 1) for v in values]
    lane = lane_iota()
    if by > 0:
        edge = lane >= LANES - by
        return [jnp.where(edge, turned[(j + 1) % count], turned[j]) for j in range(count)]
    edge = lane < -by
    return [jnp.where(edge, turned[j - 1], turned[j]) for j in range(count)]


def plus(values, others, sign=1.0):
    if others is None:
        return values
    if values is None:
        return others if sign > 0 else [-o for o in others]
    if sign > 0:
        return [v + o for v, o in zip(values, others)]
    return [v - o for v, o in zip(values, others)]


class Rows:
    def __init__(self, ref, first, rows=()):
        self.ref, self.first, self.known = ref, first, dict.fromkeys(rows)

    def get(self, row):
        if row not in self.known:
            return None
        if self.known[row] is not None:
            return self.known[row]
        return load_row(self.ref, row - self.first)

    def put(self, row, values):
        store_row(self.ref, row - self.first, values)
        self.known[row] = None


def substep(old, new, press_rows, flow_rows, east_rows, rate):
    east, flow, press = old
    new_east, new_flow, new_press = new
    every = sorted(set(press_rows) | {r + 1 for r in flow_rows} | {r + 2 for r in east_rows})
    for row in every:
        if row in press_rows:
            change = plus(flow.get(row + 1), flow.get(row - 1), -1.0)
            here = east.get(row)
            if here is not None:
                change = plus([e - b for e, b in zip(here, shifted(here, -2))], change)
            change = [rate * c for c in change]
            new_press.put(row, plus(press.get(row), change, -1.0))
        if row - 1 in flow_rows:
            slope = plus(new_press.get(row), new_press.get(row - 2), -1.0)
            new_flow.put(row - 1, plus(flow.get(row - 1), slope, -1.0))
        if row - 2 in east_rows:
            here = new_press.get(row - 2)
            slope = [a - p for a, p in zip(shifted(here, 2), here)]
            new_east.put(row - 2, plus(east.get(row - 2), slope, -1.0))


def spans(*pairs):
    return [row for low, high in pairs for row in range(low, high + 1)]


PRESS_SPANS = [
    spans((-1, 16)),
    spans((-3, 18)),
    spans((-5, 6), (9, 20)),
    spans((-5, 4), (11, 20)),
    spans((-3, 2), (13, 18)),
    spans((-1, 0), (15, 16)),
]
EAST_SPANS = [
    spans((-1, 16)),
    spans((-3, 6), (9, 18)),
    spans((-5, 4), (11, 20)),
    spans((-3, 2), (13, 18)),
    spans((-1, 0), (15, 16)),
    [],
]
FLOW_SPANS = [
    spans((-2, 17)),
    spans((-4, 19)),
    spans((-6, 5), (10, 21)),
    spans((-4, 3), (12, 19)),
    spans((-2, 1), (14, 17)),
    [],
]


def alone_kernel(
    courant,
    east_in,
    flow_in,
    press_in,
    east_0,
    flow_0,
    press_0,
    low_out,
    high_out,
    mate,
    far,
    east,
    flow,
    press,
):
    even = lax.axis_index("tile") % 2 == 0
    half = courant_half(courant)
    rate = half * half
    count = east.shape[-1] // LANES
    for block in range(2):
        rows = pl.ds(8 * block, 8)
        flow_0[rows] = jnp.swapaxes(flow_in[:, rows, :], 0, 1)
        east_0[rows] = jnp.swapaxes(east_in[:, rows, :], 0, 1)
        press_0[rows] = jnp.swapaxes(press_in[:, rows, :], 0, 1)
    inner = range(16)
    for row in inner:
        store_row(east_0, row, shifted(load_row(east_0, row), 1))
        store_row(press_0, row, [half * v for v in load_row(press_0, row)])

    def record(slot, rows):
        low, first, last, high = [rows.get(r) for r in (-1, 0, 15, 16)]
        zero = [jnp.zeros((8, LANES), F32)] * count
        store_row(low_out, slot, low or zero)
        store_row(high_out, slot, high or zero)

        @pl.when(even)
        def _():
            store_row(mate, slot, last)
            store_row(far, slot, first)

        @pl.when(jnp.logical_not(even))
        def _():
            store_row(mate, slot, first)
            store_row(far, slot, last)

    state = [Rows(ref, 0, inner) for ref in (east_0, flow_0, press_0)]
    work = [Rows(ref, -OFF) for ref in (east, flow, press)]
    for step in range(SUB):
        record(step, state[1])
        substep(
            state, work, PRESS_SPANS[step], FLOW_SPANS[step], EAST_SPANS[step], rate
        )
        state = work
        record(SUB + step, state[2])


def joined_kernel(
    n_tiles,
    courant,
    east_0,
    flow_0,
    press_0,
    low_own,
    high_own,
    from_mate,
    from_far,
    east_out,
    flow_out,
    press_out,
    east,
    flow,
    press,
):
    tile = lax.axis_index("tile")
    even = tile % 2 == 0
    half = courant_half(courant)
    rate = half * half
    inner = range(16)
    keep_low = jnp.where(tile == 0, 0.0, 1.0)
    turn = jnp.where(tile == n_tiles - 1, -1.0, 1.0)

    def border(slot, rows, sign):
        mate, far = load_row(from_mate, slot), load_row(from_far, slot)
        own_low, own_high = load_row(low_own, slot), load_row(high_own, slot)
        rows.known[-1] = [
            keep_low * o + jnp.where(even, f, m) for o, m, f in zip(own_low, mate, far)
        ]
        rows.known[16] = [
            o + sign * jnp.where(even, m, f) for o, m, f in zip(own_high, mate, far)
        ]

    state = [Rows(ref, 0, inner) for ref in (east_0, flow_0, press_0)]
    work = [Rows(ref, 0) for ref in (east, flow, press)]
    for step in range(SUB):
        border(step, state[1], turn)
        border(SUB + step, work[2], 1.0)
        substep(state, work, inner, inner, inner, rate)
        state = work
    inverse = 1.0 / half
    for row in inner:
        store_row(east, row, shifted(load_row(east, row), -1))
        store_row(press_out, row, [inverse * v for v in load_row(press, row)])
    for block in range(2):
        rows = pl.ds(8 * block, 8)
        east_out[:, rows, :] = jnp.swapaxes(east[rows], 0, 1)
        flow_out[:, rows, :] = jnp.swapaxes(flow[rows], 0, 1)


def spread_kernel(press, heat_own, heat_back, out, heat_rows, sums):
    even_lane = lane_iota() % 2 == 0
    for source, part in enumerate((heat_own, heat_back)):
        width = part.shape[-1]
        heat_rows[:, :, pl.ds(source * width, width)] = jnp.swapaxes(part[...], 0, 1)
    for sublane in range(8):
        coarse = sublane // 2 + 4 * (sublane % 2)
        for block, value in enumerate(load_row(heat_rows, sublane)):
            left = jnp.where(even_lane, value, pltpu.roll(value, 1, 1))
            right = jnp.where(even_lane, pltpu.roll(value, LANES - 1, 1), value)
            for side, heat in enumerate((left, right)):
                cols = pl.ds((2 * block + side) * LANES, LANES)
                for row in (2 * coarse, 2 * coarse + 1):
                    sums[row, :, cols] = press[row, :, cols] + heat
    for block in range(2):
        rows = pl.ds(8 * block, 8)
        out[:, rows, :] = jnp.swapaxes(sums[rows], 0, 1)


def call(kernel, outs, n_smem, n_vmem, scratch=(), limit=16):
    return pl.pallas_call(
        kernel,
        out_shape=[jax.ShapeDtypeStruct(s, F32) for s in outs],
        in_specs=[pl.BlockSpec(memory_space=SMEM)] * n_smem
        + [pl.BlockSpec(memory_space=VMEM)] * n_vmem,
        out_specs=[pl.BlockSpec(memory_space=VMEM)] * len(outs),
        scratch_shapes=[VMEM(s, F32) for s in scratch],
        compiler_params=pltpu.CompilerParams(vmem_limit_bytes=limit << 20),
        cost_estimate=pl.CostEstimate(
            flops=10**7, bytes_accessed=10**7, transcendentals=0
        ),
    )


def shards(
    east_wind, equator_wind, pressure, moisture, albedo, courant, sun_angles, absorption, solar_weights
):
    east, flow, press, moist = east_wind[0], equator_wind[0], pressure[0], moisture[0]
    levels, rows, cols = east.shape
    n_tiles = lax.axis_size("tile")
    half_cols = cols // 4
    swap = [(0, 1), (1, 0)]

    def both_ways(pairs):
        return [pair for a, b in pairs for pair in ((a, b), (b, a))]

    mates = both_ways((t, t + 1) for t in range(0, n_tiles, 2))
    fars = both_ways(
        [
            (g * n_tiles + t, g * n_tiles + t + 1)
            for g in range(2)
            for t in range(1, n_tiles - 1, 2)
        ]
        + [(n_tiles - 1, 2 * n_tiles - 1)]
    )

    coarse = (9, 8, half_cols)
    keep, send = call(coarsen_kernel, [coarse, coarse], 0, 2)(moist, albedo[0])
    other = lax.ppermute(send, "group", swap)

    series = (2 * SUB, 8, cols)
    staged = (rows, 8, cols)
    east, flow, press, low, high, mate, far = call(
        alone_kernel, [staged] * 3 + [series] * 4, 1, 3, [(rows + 2 * OFF, 8, cols)] * 3
    )(courant, east, flow, press)
    from_far = lax.ppermute(far, ("group", "tile"), fars)
    from_mate = lax.ppermute(mate, "tile", mates)

    heat = (8, 8, half_cols)
    heat_own, heat_other = call(
        functools.partial(radiate_kernel, n_tiles * rows // 2, cols // 2),
        [heat, heat],
        3,
        2,
    )(sun_angles, absorption, solar_weights, keep, other)
    heat_back = lax.ppermute(heat_other, "group", swap)

    field = (levels, rows, cols)
    east, flow, press = call(
        functools.partial(joined_kernel, n_tiles),
        [field, field, staged],
        1,
        7,
        [staged] * 3,
    )(courant, east, flow, press, low, high, from_mate, from_far)
    (press,) = call(
        spread_kernel, [field], 0, 3, [(8, 8, cols // 2), staged]
    )(press, heat_own, heat_back)
    return east[None], flow[None], press[None]


def solution(mesh):
    field = P("group", None, "tile", None)
    return jax.shard_map(
        shards,
        mesh=mesh,
        in_specs=(field,) * 4 + (P("group", "tile", None),) + (P(),) * 4,
        out_specs=(field,) * 3,
        check_vma=False,
    )
```

```python
import functools
import math

import jax
import jax.numpy as jnp
from jax import lax
from jax.experimental import pallas as pl
from jax.experimental.pallas import tpu as pltpu
from jax.sharding import PartitionSpec as P


SUB = 6
HEAT_SCALE = 10.0
MU_OFFSET = 0.1
DIFFUSE = 1.66
LOG2E = 1.4426950408889634
LANES = 128
OFF = 8

VMEM = pltpu.VMEM
SMEM = pltpu.SMEM
HBM = pltpu.HBM
F32 = jnp.float32


def lane_iota(dtype=jnp.int32):
    return lax.broadcasted_iota(dtype, (8, LANES), 1)


def sub_iota():
    return lax.broadcasted_iota(jnp.int32, (8, LANES), 0)


def coarsen(moist, albedo, keep, send):
    width = moist.shape[-1]
    half = keep.shape[-1] // LANES
    even_row = sub_iota() % 2 == 0
    even_lane = lane_iota() % 2 == 0

    def fold(top, bottom):
        return jnp.where(
            even_row, top + pltpu.roll(top, 7, 0), bottom + pltpu.roll(bottom, 1, 0)
        )

    def pack(left, right):
        return jnp.where(
            even_lane,
            left + pltpu.roll(left, LANES - 1, 1),
            right + pltpu.roll(right, 1, 1),
        )

    for level in range(9):
        for block in range(width // (2 * LANES)):
            parts = []
            for side in range(2):
                cols = pl.ds((2 * block + side) * LANES, LANES)
                source = moist if level < 8 else albedo
                index = (level,) if level < 8 else ()
                parts.append((source[(*index, slice(0, 8), cols)], source[(*index, slice(8, 16), cols)]))
            top = pack(parts[0][0], parts[1][0])
            bottom = pack(parts[0][1], parts[1][1])
            value = fold(top, bottom) * 0.25
            if block < half:
                keep[level, :, pl.ds(block * LANES, LANES)] = value
            else:
                send[level, :, pl.ds((block - half) * LANES, LANES)] = value


def turn_in(source, rows, target, turned, scale=None):
    by_row = jnp.swapaxes(source[:, pl.ds(rows, 8), :], 0, 1)
    for row in range(8):
        blocks = [by_row[row][:, b * LANES : (b + 1) * LANES] for b in range(16)]
        turned[rows + row] = jnp.concatenate(blocks, axis=0).T
        for i in range(16):
            value = turned[rows + row, pl.ds(i, 8, stride=16), :]
            if scale is not None:
                value = scale * value
            target[rows + row, pl.ds(8 * i, 8), :] = value


def turn_out(source, rows, target, turned, by_row, scale=None):
    for row in range(rows, rows + 8):
        for i in range(16):
            value = source[row, pl.ds(8 * i, 8), :]
            if scale is not None:
                value = scale * value
            turned[row, pl.ds(i, 8, stride=16), :] = value
        blocks = turned[row].T
        for b in range(16):
            by_row[row, :, pl.ds(b * LANES, LANES)] = blocks[8 * b : 8 * b + 8]
    target[:, pl.ds(rows, 8), :] = jnp.swapaxes(by_row[pl.ds(rows, 8)], 0, 1)


def prepare_kernel(
    courant_in,
    moist_in,
    albedo_in,
    east_in,
    flow_in,
    press_in,
    keep,
    send,
    east_0,
    flow_0,
    press_0,
    moist,
    albedo,
    east,
    flow,
    press,
    turned,
    sems,
    courant,
):
    pairs = [(moist_in, moist), (flow_in, flow), (east_in, east), (press_in, press)]
    parts = 4
    copies = {}
    for n, (source, target) in enumerate(pairs):
        for part in range(parts):
            some = pl.ds(2 * part, 2)
            copies[n, part] = pltpu.make_async_copy(
                source.at[some], target.at[some], sems.at[n, part]
            )
        if n == 0:
            copies[4, 0] = pltpu.make_async_copy(albedo_in, albedo, sems.at[4, 0])
    copies[5, 0] = pltpu.make_async_copy(courant_in, courant, sems.at[4, 1])
    for copy in copies.values():
        copy.start()

    def wait(n):
        for (field, _), copy in copies.items():
            if field == n:
                copy.wait()

    wait(0)
    wait(4)
    coarsen(moist, albedo, keep, send)
    wait(5)
    half = courant_half(courant)
    for n, field, target, scale in (
        (1, flow, flow_0, None),
        (2, east, east_0, None),
        (3, press, press_0, half),
    ):
        wait(n)
        for rows in (0, 8):
            turn_in(field, rows, target, turned, scale)


def radiate_kernel(
    rows_total, cols_total, sun, absorption, weights, own, other, heat_own, heat_other
):
    group = lax.axis_index("group")
    tile = lax.axis_index("tile")
    sublane = sub_iota()
    lane = lane_iota()
    row = tile * 8 + sublane // 2 + 4 * (sublane % 2)
    colatitude = 1.0 - (row.astype(F32) + 0.5) / rows_total
    hemisphere = 2.0 * group.astype(F32) - 1.0
    latitude = hemisphere * (0.5 * math.pi) * colatitude
    declination = 0.41 * jnp.sin(jnp.full((8, LANES), sun[0], F32))
    sine = jnp.sin(latitude) * jnp.sin(declination)
    cosine = jnp.cos(latitude) * jnp.cos(declination)
    n_g = absorption.shape[0]

    for block in range(own.shape[-1] // LANES):
        cols = pl.ds(block * LANES, LANES)
        column = block * LANES + lane // 2 + 64 * (lane % 2)
        longitude = 2.0 * math.pi * (column.astype(F32) + 0.5) / cols_total
        mu = sine + cosine * jnp.cos(longitude - sun[1])
        lit = mu > 0.0
        sunlit = jnp.abs(mu)
        slant = 1.0 / (sunlit + MU_OFFSET)
        depth = [jnp.zeros((8, LANES), F32)]
        for level in range(8):
            layer = jnp.where(lit, own[level, :, cols], other[level, :, cols])
            depth.append(depth[-1] + layer)
        surface = jnp.where(lit, own[8, :, cols], other[8, :, cols])
        total = depth[8]
        direct = total * slant
        paths = [depth[j] * slant for j in range(1, 9)]
        paths += [direct + DIFFUSE * (total - depth[j]) for j in range(8)]

        def body(g, carry):
            rate = absorption[g] * (-LOG2E)
            weight = weights[g]
            sums, whole = carry[:-1], carry[-1]
            sums = tuple(a + weight * jnp.exp2(rate * p) for a, p in zip(sums, paths))
            return sums + (whole + weight,)

        zero = jnp.zeros((8, LANES), F32)
        sums = lax.fori_loop(0, n_g, body, (zero,) * 17, unroll=32)
        down = (sums[16],) + sums[:8]
        up = sums[8:16] + (sums[7],)
        scale = sunlit * (HEAT_SCALE / n_g)
        net = [scale * (down[j] - surface * up[j]) for j in range(9)]
        for level in range(8):
            heat = net[level] - net[level + 1]
            heat_own[level, :, cols] = jnp.where(lit, heat, 0.0)
            heat_other[level, :, cols] = jnp.where(lit, 0.0, heat)


def courant_half(courant):
    level = lane_iota() % 8
    value = jnp.full((8, LANES), courant[7], F32)
    for index in range(7):
        value = jnp.where(level == index, courant[index], value)
    return 0.5 * value


def load_row(ref, row):
    return [ref[row, pl.ds(8 * i, 8), :] for i in range(16)]


def store_row(ref, row, values):
    for i, value in enumerate(values):
        if value is not None:
            ref[row, pl.ds(8 * i, 8), :] = value


def past_end(first):
    up = pltpu.roll(first, 7, 0)
    return jnp.where(sub_iota() == 7, pltpu.roll(up, LANES - 8, 1), up)


def before_start(last):
    down = pltpu.roll(last, 1, 0)
    return jnp.where(sub_iota() == 0, pltpu.roll(down, 8, 1), down)


def plus(values, others, sign=1.0):
    if others is None:
        return values
    if values is None:
        return others if sign > 0 else [-o for o in others]
    if sign > 0:
        return [v + o for v, o in zip(values, others)]
    return [v - o for v, o in zip(values, others)]


class Rows:
    def __init__(self, ref, first, rows=()):
        self.ref, self.first, self.known = ref, first, dict.fromkeys(rows)

    def get(self, row):
        if row not in self.known:
            return None
        if self.known[row] is not None:
            return self.known[row]
        return load_row(self.ref, row - self.first)

    def put(self, row, values):
        store_row(self.ref, row - self.first, values)
        self.known[row] = None


def substep(old, new, press_rows, flow_rows, east_rows, rate):
    east, flow, press = old
    new_east, new_flow, new_press = new
    every = sorted(set(press_rows) | {r + 1 for r in flow_rows})
    waiting = []

    def ends():
        row, before, after, pressures, winds = waiting.pop(0)
        low, high = pressures[0] - before, after - pressures[1]
        if winds is not None:
            low, high = winds[0] - low, winds[1] - high
        else:
            low, high = -low, -high
        new_east.put(row, [low] + [None] * 14 + [high])

    for row in every:
        if row in press_rows:
            change = plus(flow.get(row + 1), flow.get(row - 1), -1.0)
            winds = east.get(row)
            if winds is not None:
                ahead = winds[1:] + [past_end(winds[0])]
                behind = [before_start(winds[15])] + winds[:-1]
                change = plus([a - b for a, b in zip(ahead, behind)], change)
            change = [rate * c for c in change]
            here = plus(press.get(row), change, -1.0)
            new_press.put(row, here)
            if row in east_rows:
                slope = [here[i + 1] - here[i - 1] for i in range(1, 15)]
                inside = plus(winds and winds[1:15], slope, -1.0)
                new_east.put(row, [None] + inside + [None])
                waiting.append(
                    (
                        row,
                        before_start(here[15]),
                        past_end(here[0]),
                        (here[1], here[14]),
                        winds and (winds[0], winds[15]),
                    )
                )
        if row - 1 in flow_rows:
            slope = plus(new_press.get(row), new_press.get(row - 2), -1.0)
            new_flow.put(row - 1, plus(flow.get(row - 1), slope, -1.0))
        if len(waiting) > 2:
            ends()
    while waiting:
        ends()


def spans(*pairs):
    return [row for low, high in pairs for row in range(low, high + 1)]


PRESS_SPANS = [
    spans((-1, 16)),
    spans((-3, 18)),
    spans((-5, 6), (9, 20)),
    spans((-5, 4), (11, 20)),
    spans((-3, 2), (13, 18)),
    spans((-1, 0), (15, 16)),
]
EAST_SPANS = [
    spans((-1, 16)),
    spans((-3, 6), (9, 18)),
    spans((-5, 4), (11, 20)),
    spans((-3, 2), (13, 18)),
    spans((-1, 0), (15, 16)),
    [],
]
FLOW_SPANS = [
    spans((-2, 17)),
    spans((-4, 19)),
    spans((-6, 5), (10, 21)),
    spans((-4, 3), (12, 19)),
    spans((-2, 1), (14, 17)),
    [],
]


def alone_kernel(
    courant, east_0, flow_0, press_0, low_out, high_out, mate, far, east, flow, press
):
    even = lax.axis_index("tile") % 2 == 0
    half = courant_half(courant)
    rate = half * half
    inner = range(16)

    def record(slot, rows):
        low, first, last, high = [rows.get(r) for r in (-1, 0, 15, 16)]
        zero = [jnp.zeros((8, LANES), F32)] * 16
        store_row(low_out, slot, low or zero)
        store_row(high_out, slot, high or zero)

        @pl.when(even)
        def _():
            store_row(mate, slot, last)
            store_row(far, slot, first)

        @pl.when(jnp.logical_not(even))
        def _():
            store_row(mate, slot, first)
            store_row(far, slot, last)

    state = [Rows(ref, 0, inner) for ref in (east_0, flow_0, press_0)]
    work = [Rows(ref, -OFF) for ref in (east, flow, press)]
    for step in range(SUB):
        record(step, state[1])
        substep(
            state, work, PRESS_SPANS[step], FLOW_SPANS[step], EAST_SPANS[step], rate
        )
        state = work
        record(SUB + step, state[2])


def joined_kernel(
    n_tiles,
    courant,
    east_0,
    flow_0,
    press_0,
    low_own,
    high_own,
    from_mate,
    from_far,
    east_out,
    flow_out,
    press_out,
    east,
    flow,
    press,
    turned,
    by_row,
    ready_east,
    ready_flow,
    sems,
):
    tile = lax.axis_index("tile")
    even = tile % 2 == 0
    half = courant_half(courant)
    rate = half * half
    inner = range(16)
    keep_low = jnp.where(tile == 0, 0.0, 1.0)
    turn = jnp.where(tile == n_tiles - 1, -1.0, 1.0)

    def border(slot, rows, sign):
        mate, far = load_row(from_mate, slot), load_row(from_far, slot)
        own_low, own_high = load_row(low_own, slot), load_row(high_own, slot)
        rows.known[-1] = [
            keep_low * o + jnp.where(even, f, m) for o, m, f in zip(own_low, mate, far)
        ]
        rows.known[16] = [
            o + sign * jnp.where(even, m, f) for o, m, f in zip(own_high, mate, far)
        ]

    state = [Rows(ref, 0, inner) for ref in (east_0, flow_0, press_0)]
    work = [Rows(ref, 0) for ref in (east, flow, press)]
    for step in range(SUB):
        border(step, state[1], turn)
        border(SUB + step, work[2], 1.0)
        substep(state, work, inner, inner, inner, rate)
        state = work
    copies = []
    for field, ready, out in (
        (flow, ready_flow, flow_out),
        (east, ready_east, east_out),
    ):
        for rows in (0, 8):
            turn_out(field, rows, ready, turned, by_row)
            some = pl.ds(rows, 8)
            copies.append(
                pltpu.make_async_copy(
                    ready.at[:, some], out.at[:, some], sems.at[len(copies)]
                )
            )
            copies[-1].start()
    for rows in (0, 8):
        turn_out(press, rows, press_out, turned, by_row, 1.0 / half)
    for copy in copies:
        copy.wait()


def spread_kernel(press, heat_own, heat_back, out, ready, sems):
    even_lane = lane_iota() % 2 == 0
    even_row = sub_iota() % 2 == 0
    blocks = heat_own.shape[-1] // LANES
    copies = []
    for level in range(8):
        for block in range(2 * blocks):
            part = heat_own if block < blocks else heat_back
            value = part[level, :, pl.ds(block % blocks * LANES, LANES)]
            left = jnp.where(even_lane, value, pltpu.roll(value, 1, 1))
            right = jnp.where(even_lane, pltpu.roll(value, LANES - 1, 1), value)
            for side, heat in enumerate((left, right)):
                cols = pl.ds((2 * block + side) * LANES, LANES)
                top = jnp.where(even_row, heat, pltpu.roll(heat, 1, 0))
                bottom = jnp.where(even_row, pltpu.roll(heat, 7, 0), heat)
                ready[level, 0:8, cols] = press[level, 0:8, cols] + top
                ready[level, 8:16, cols] = press[level, 8:16, cols] + bottom
        copies.append(
            pltpu.make_async_copy(ready.at[level], out.at[level], sems.at[level])
        )
        copies[-1].start()
    for copy in copies:
        copy.wait()


def call(kernel, ins, outs, scratch=(), sems=None, more=(), limit=16):
    return pl.pallas_call(
        kernel,
        out_shape=[jax.ShapeDtypeStruct(shape, F32) for shape, _ in outs],
        in_specs=[pl.BlockSpec(memory_space=space) for space in ins],
        out_specs=[pl.BlockSpec(memory_space=space) for _, space in outs],
        scratch_shapes=[VMEM(shape, F32) for shape in scratch]
        + ([pltpu.SemaphoreType.DMA(sems)] if sems else [])
        + list(more),
        compiler_params=pltpu.CompilerParams(vmem_limit_bytes=limit << 20),
        cost_estimate=pl.CostEstimate(
            flops=10**7, bytes_accessed=10**7, transcendentals=0
        ),
    )


def shards(
    east_wind, equator_wind, pressure, moisture, albedo, courant, sun_angles, absorption, solar_weights
):
    east, flow, press, moist = east_wind[0], equator_wind[0], pressure[0], moisture[0]
    levels, rows, cols = east.shape
    n_tiles = lax.axis_size("tile")
    half_cols = cols // 4
    swap = [(0, 1), (1, 0)]

    def both_ways(pairs):
        return [pair for a, b in pairs for pair in ((a, b), (b, a))]

    mates = both_ways((t, t + 1) for t in range(0, n_tiles, 2))
    fars = both_ways(
        [
            (g * n_tiles + t, g * n_tiles + t + 1)
            for g in range(2)
            for t in range(1, n_tiles - 1, 2)
        ]
        + [(n_tiles - 1, 2 * n_tiles - 1)]
    )

    field = (levels, rows, cols)
    coarse = (9, 8, half_cols)
    staged = (rows, LANES, LANES)
    series = (2 * SUB, LANES, LANES)
    heat = (8, 8, half_cols)

    keep, send, east, flow, press = call(
        prepare_kernel,
        [HBM] * 6,
        [(coarse, VMEM)] * 2 + [(staged, VMEM)] * 3,
        [field, albedo.shape[1:], field, field, field, staged],
        (5, 4),
        [SMEM(courant.shape, F32)],
    )(
        *(
            pltpu.with_memory_space_constraint(x, HBM)
            for x in (courant, moist, albedo[0], east, flow, press)
        )
    )
    other = lax.ppermute(send, "group", swap)

    low, high, mate, far = call(
        alone_kernel,
        [SMEM] + [VMEM] * 3,
        [(series, VMEM)] * 4,
        [(rows + 2 * OFF, LANES, LANES)] * 3,
    )(courant, east, flow, press)
    from_far = lax.ppermute(far, ("group", "tile"), fars)
    from_mate = lax.ppermute(mate, "tile", mates)

    heat_own, heat_other = call(
        functools.partial(radiate_kernel, n_tiles * rows // 2, cols // 2),
        [SMEM] * 3 + [VMEM] * 2,
        [(heat, VMEM)] * 2,
    )(sun_angles, absorption, solar_weights, keep, other)
    heat_back = lax.ppermute(heat_other, "group", swap)

    east, flow, press = call(
        functools.partial(joined_kernel, n_tiles),
        [SMEM] + [VMEM] * 7,
        [(field, HBM)] * 2 + [(field, VMEM)],
        [staged] * 4 + [(rows, 8, cols)] + [field] * 2,
        (4,),
    )(courant, east, flow, press, low, high, from_mate, from_far)
    (press,) = call(
        spread_kernel, [VMEM] * 3, [(field, HBM)], [field], (8,)
    )(press, heat_own, heat_back)
    return east[None], flow[None], press[None]


def solution(mesh):
    field = P("group", None, "tile", None)
    return jax.shard_map(
        shards,
        mesh=mesh,
        in_specs=(field,) * 4 + (P("group", "tile", None),) + (P(),) * 4,
        out_specs=(field,) * 3,
        check_vma=False,
    )
```

```python
import functools
import math

import jax
import jax.numpy as jnp
from jax import lax
from jax.experimental import pallas as pl
from jax.experimental.pallas import tpu as pltpu
from jax.sharding import PartitionSpec as P


SUB = 6
HEAT_SCALE = 10.0
MU_OFFSET = 0.1
DIFFUSE = 1.66
LOG2E = 1.4426950408889634
LANES = 128
OFF = 8

VMEM = pltpu.VMEM
SMEM = pltpu.SMEM
HBM = pltpu.HBM
F32 = jnp.float32


def lane_iota(dtype=jnp.int32):
    return lax.broadcasted_iota(dtype, (8, LANES), 1)


def sub_iota():
    return lax.broadcasted_iota(jnp.int32, (8, LANES), 0)


def coarsen(moist, albedo, keep, send):
    width = moist.shape[-1]
    half = keep.shape[-1] // LANES
    even_row = sub_iota() % 2 == 0
    even_lane = lane_iota() % 2 == 0

    def fold(top, bottom):
        return jnp.where(
            even_row, top + pltpu.roll(top, 7, 0), bottom + pltpu.roll(bottom, 1, 0)
        )

    def pack(left, right):
        return jnp.where(
            even_lane,
            left + pltpu.roll(left, LANES - 1, 1),
            right + pltpu.roll(right, 1, 1),
        )

    for level in range(9):
        for block in range(width // (2 * LANES)):
            parts = []
            for side in range(2):
                cols = pl.ds((2 * block + side) * LANES, LANES)
                source = moist if level < 8 else albedo
                index = (level,) if level < 8 else ()
                parts.append((source[(*index, slice(0, 8), cols)], source[(*index, slice(8, 16), cols)]))
            top = pack(parts[0][0], parts[1][0])
            bottom = pack(parts[0][1], parts[1][1])
            value = fold(top, bottom) * 0.25
            if block < half:
                keep[level, :, pl.ds(block * LANES, LANES)] = value
            else:
                send[level, :, pl.ds((block - half) * LANES, LANES)] = value


def turn_in(source, rows, target, turned, scale=None):
    by_row = jnp.swapaxes(source[:, pl.ds(rows, 8), :], 0, 1)
    for row in range(8):
        blocks = [by_row[row][:, b * LANES : (b + 1) * LANES] for b in range(16)]
        turned[rows + row] = jnp.concatenate(blocks, axis=0).T
        for i in range(16):
            value = turned[rows + row, pl.ds(i, 8, stride=16), :]
            if scale is not None:
                value = scale * value
            target[rows + row, pl.ds(8 * i, 8), :] = value


def turn_out(source, rows, target, turned, by_row, scale=None):
    for row in range(rows, rows + 8):
        for i in range(16):
            value = source[row, pl.ds(8 * i, 8), :]
            if scale is not None:
                value = scale * value
            turned[row, pl.ds(i, 8, stride=16), :] = value
        blocks = turned[row].T
        for b in range(16):
            by_row[row, :, pl.ds(b * LANES, LANES)] = blocks[8 * b : 8 * b + 8]
    target[:, pl.ds(rows, 8), :] = jnp.swapaxes(by_row[pl.ds(rows, 8)], 0, 1)


def prepare_kernel(
    courant_in,
    moist_in,
    albedo_in,
    east_in,
    flow_in,
    press_in,
    keep,
    send,
    east_0,
    flow_0,
    press_0,
    half_out,
    moist,
    albedo,
    east,
    flow,
    press,
    turned,
    sems,
    courant,
):
    fields = [(flow_in, flow), (east_in, east), (press_in, press)]
    copies = {("courant", 0): pltpu.make_async_copy(courant_in, courant, sems.at[0, 0])}
    for n, (source, target) in enumerate(fields):
        for part in range(4):
            some = (pl.ds(part % 2 * 4, 4), pl.ds(part // 2 * 8, 8))
            copies[n, part // 2, part % 2] = pltpu.make_async_copy(
                source.at[some], target.at[some], sems.at[n + 1, part]
            )
    for part in range(4):
        some = pl.ds(2 * part, 2)
        copies["coarse", part] = pltpu.make_async_copy(
            moist_in.at[some], moist.at[some], sems.at[4, part]
        )
    copies["coarse", 4] = pltpu.make_async_copy(albedo_in, albedo, sems.at[0, 1])
    for copy in copies.values():
        copy.start()

    def wait(*key):
        for name, copy in copies.items():
            if name[: len(key)] == key:
                copy.wait()

    wait("courant")
    half = courant_half(courant)
    half_out[...] = half
    for n, (field, target, scale) in enumerate(
        ((flow, flow_0, None), (east, east_0, None), (press, press_0, half))
    ):
        for part in range(2):
            wait(n, part)
            turn_in(field, 8 * part, target, turned, scale)
    wait("coarse")
    coarsen(moist, albedo, keep, send)


def radiate_kernel(
    rows_total, cols_total, sun, absorption, weights, own, other, heat_own, heat_other
):
    group = lax.axis_index("group")
    tile = lax.axis_index("tile")
    sublane = sub_iota()
    lane = lane_iota()
    row = tile * 8 + sublane // 2 + 4 * (sublane % 2)
    colatitude = 1.0 - (row.astype(F32) + 0.5) / rows_total
    hemisphere = 2.0 * group.astype(F32) - 1.0
    latitude = hemisphere * (0.5 * math.pi) * colatitude
    declination = 0.41 * jnp.sin(jnp.full((8, LANES), sun[0], F32))
    sine = jnp.sin(latitude) * jnp.sin(declination)
    cosine = jnp.cos(latitude) * jnp.cos(declination)
    n_g = absorption.shape[0]

    for block in range(own.shape[-1] // LANES):
        cols = pl.ds(block * LANES, LANES)
        column = block * LANES + lane // 2 + 64 * (lane % 2)
        longitude = 2.0 * math.pi * (column.astype(F32) + 0.5) / cols_total
        mu = sine + cosine * jnp.cos(longitude - sun[1])
        lit = mu > 0.0
        sunlit = jnp.abs(mu)
        slant = 1.0 / (sunlit + MU_OFFSET)
        depth = [jnp.zeros((8, LANES), F32)]
        for level in range(8):
            layer = jnp.where(lit, own[level, :, cols], other[level, :, cols])
            depth.append(depth[-1] + layer)
        surface = jnp.where(lit, own[8, :, cols], other[8, :, cols])
        total = depth[8]
        direct = total * slant
        paths = [depth[j] * slant for j in range(1, 9)]
        paths += [direct + DIFFUSE * (total - depth[j]) for j in range(8)]

        def body(g, carry):
            rate = absorption[g] * (-LOG2E)
            weight = weights[g]
            sums, whole = carry[:-1], carry[-1]
            sums = tuple(a + weight * jnp.exp2(rate * p) for a, p in zip(sums, paths))
            return sums + (whole + weight,)

        zero = jnp.zeros((8, LANES), F32)
        sums = lax.fori_loop(0, n_g, body, (zero,) * 17, unroll=32)
        down = (sums[16],) + sums[:8]
        up = sums[8:16] + (sums[7],)
        scale = sunlit * (HEAT_SCALE / n_g)
        net = [scale * (down[j] - surface * up[j]) for j in range(9)]
        for level in range(8):
            heat = net[level] - net[level + 1]
            heat_own[level, :, cols] = jnp.where(lit, heat, 0.0)
            heat_other[level, :, cols] = jnp.where(lit, 0.0, heat)


def courant_half(courant):
    level = lane_iota() % 8
    value = jnp.full((8, LANES), courant[7], F32)
    for index in range(7):
        value = jnp.where(level == index, courant[index], value)
    return 0.5 * value


def load_row(ref, row):
    return [ref[row, pl.ds(8 * i, 8), :] for i in range(16)]


def store_row(ref, row, values):
    for i, value in enumerate(values):
        if value is not None:
            ref[row, pl.ds(8 * i, 8), :] = value


def past_end(first):
    up = pltpu.roll(first, 7, 0)
    return jnp.where(sub_iota() == 7, pltpu.roll(up, LANES - 8, 1), up)


def before_start(last):
    down = pltpu.roll(last, 1, 0)
    return jnp.where(sub_iota() == 0, pltpu.roll(down, 8, 1), down)


def plus(values, others, sign=1.0):
    if others is None:
        return values
    if values is None:
        return others if sign > 0 else [-o for o in others]
    if sign > 0:
        return [v + o for v, o in zip(values, others)]
    return [v - o for v, o in zip(values, others)]


class Rows:
    def __init__(self, ref, first, rows=()):
        self.ref, self.first, self.known = ref, first, dict.fromkeys(rows)

    def get(self, row):
        if row not in self.known:
            return None
        if self.known[row] is not None:
            return self.known[row]
        return load_row(self.ref, row - self.first)

    def put(self, row, values):
        store_row(self.ref, row - self.first, values)
        self.known[row] = None


def substep(old, new, press_rows, flow_rows, east_rows, rate):
    east, flow, press = old
    new_east, new_flow, new_press = new
    every = sorted(set(press_rows) | {r + 1 for r in flow_rows})
    waiting = []

    def ends():
        row, before, after, pressures, winds = waiting.pop(0)
        low, high = pressures[0] - before, after - pressures[1]
        if winds is not None:
            low, high = winds[0] - low, winds[1] - high
        else:
            low, high = -low, -high
        new_east.put(row, [low] + [None] * 14 + [high])

    for row in every:
        if row in press_rows:
            change = plus(flow.get(row + 1), flow.get(row - 1), -1.0)
            winds = east.get(row)
            if winds is not None:
                ahead = winds[1:] + [past_end(winds[0])]
                behind = [before_start(winds[15])] + winds[:-1]
                change = plus([a - b for a, b in zip(ahead, behind)], change)
            change = [rate * c for c in change]
            here = plus(press.get(row), change, -1.0)
            new_press.put(row, here)
            if row in east_rows:
                slope = [here[i + 1] - here[i - 1] for i in range(1, 15)]
                inside = plus(winds and winds[1:15], slope, -1.0)
                new_east.put(row, [None] + inside + [None])
                waiting.append(
                    (
                        row,
                        before_start(here[15]),
                        past_end(here[0]),
                        (here[1], here[14]),
                        winds and (winds[0], winds[15]),
                    )
                )
        if row - 1 in flow_rows:
            slope = plus(new_press.get(row), new_press.get(row - 2), -1.0)
            new_flow.put(row - 1, plus(flow.get(row - 1), slope, -1.0))
        if len(waiting) > 2:
            ends()
    while waiting:
        ends()


def spans(*pairs):
    return [row for low, high in pairs for row in range(low, high + 1)]


PRESS_SPANS = [
    spans((-1, 16)),
    spans((-3, 18)),
    spans((-5, 6), (9, 20)),
    spans((-5, 4), (11, 20)),
    spans((-3, 2), (13, 18)),
    spans((-1, 0), (15, 16)),
]
EAST_SPANS = [
    spans((-1, 16)),
    spans((-3, 6), (9, 18)),
    spans((-5, 4), (11, 20)),
    spans((-3, 2), (13, 18)),
    spans((-1, 0), (15, 16)),
    [],
]
FLOW_SPANS = [
    spans((-2, 17)),
    spans((-4, 19)),
    spans((-6, 5), (10, 21)),
    spans((-4, 3), (12, 19)),
    spans((-2, 1), (14, 17)),
    [],
]


def alone_kernel(
    half, east_0, flow_0, press_0, low_out, high_out, mate, far, east, flow, press
):
    even = lax.axis_index("tile") % 2 == 0
    rate = half[...] * half[...]
    inner = range(16)

    def record(slot, rows):
        low, first, last, high = [rows.get(r) for r in (-1, 0, 15, 16)]
        zero = [jnp.zeros((8, LANES), F32)] * 16
        store_row(low_out, slot, low or zero)
        store_row(high_out, slot, high or zero)

        @pl.when(even)
        def _():
            store_row(mate, slot, last)
            store_row(far, slot, first)

        @pl.when(jnp.logical_not(even))
        def _():
            store_row(mate, slot, first)
            store_row(far, slot, last)

    state = [Rows(ref, 0, inner) for ref in (east_0, flow_0, press_0)]
    work = [Rows(ref, -OFF) for ref in (east, flow, press)]
    for step in range(SUB):
        record(step, state[1])
        substep(
            state, work, PRESS_SPANS[step], FLOW_SPANS[step], EAST_SPANS[step], rate
        )
        state = work
        record(SUB + step, state[2])


def joined_kernel(
    n_tiles,
    half,
    east_0,
    flow_0,
    press_0,
    low_own,
    high_own,
    from_mate,
    from_far,
    east_out,
    flow_out,
    press_out,
    east,
    flow,
    press,
    turned,
    by_row,
    ready_east,
    ready_flow,
    sems,
):
    tile = lax.axis_index("tile")
    even = tile % 2 == 0
    rate = half[...] * half[...]
    inner = range(16)
    keep_low = jnp.where(tile == 0, 0.0, 1.0)
    turn = jnp.where(tile == n_tiles - 1, -1.0, 1.0)

    def border(slot, rows, sign):
        mate, far = load_row(from_mate, slot), load_row(from_far, slot)
        own_low, own_high = load_row(low_own, slot), load_row(high_own, slot)
        rows.known[-1] = [
            keep_low * o + jnp.where(even, f, m) for o, m, f in zip(own_low, mate, far)
        ]
        rows.known[16] = [
            o + sign * jnp.where(even, m, f) for o, m, f in zip(own_high, mate, far)
        ]

    state = [Rows(ref, 0, inner) for ref in (east_0, flow_0, press_0)]
    work = [Rows(ref, 0) for ref in (east, flow, press)]
    for step in range(SUB):
        border(step, state[1], turn)
        border(SUB + step, work[2], 1.0)
        substep(state, work, inner, inner, inner, rate)
        state = work
    copies = []
    for field, ready, out in (
        (flow, ready_flow, flow_out),
        (east, ready_east, east_out),
    ):
        for rows in (0, 8):
            turn_out(field, rows, ready, turned, by_row)
            some = pl.ds(rows, 8)
            copies.append(
                pltpu.make_async_copy(
                    ready.at[:, some], out.at[:, some], sems.at[len(copies)]
                )
            )
            copies[-1].start()
    for rows in (0, 8):
        turn_out(press, rows, press_out, turned, by_row, 1.0 / half[...])
    for copy in copies:
        copy.wait()


def spread_kernel(press, heat_own, heat_back, out, ready, sems):
    even_lane = lane_iota() % 2 == 0
    even_row = sub_iota() % 2 == 0
    blocks = heat_own.shape[-1] // LANES
    copies = []
    for level in range(8):
        for block in range(2 * blocks):
            part = heat_own if block < blocks else heat_back
            value = part[level, :, pl.ds(block % blocks * LANES, LANES)]
            left = jnp.where(even_lane, value, pltpu.roll(value, 1, 1))
            right = jnp.where(even_lane, pltpu.roll(value, LANES - 1, 1), value)
            for side, heat in enumerate((left, right)):
                cols = pl.ds((2 * block + side) * LANES, LANES)
                top = jnp.where(even_row, heat, pltpu.roll(heat, 1, 0))
                bottom = jnp.where(even_row, pltpu.roll(heat, 7, 0), heat)
                ready[level, 0:8, cols] = press[level, 0:8, cols] + top
                ready[level, 8:16, cols] = press[level, 8:16, cols] + bottom
        copies.append(
            pltpu.make_async_copy(ready.at[level], out.at[level], sems.at[level])
        )
        copies[-1].start()
    for copy in copies:
        copy.wait()


def call(kernel, ins, outs, scratch=(), sems=None, more=(), limit=16):
    return pl.pallas_call(
        kernel,
        out_shape=[jax.ShapeDtypeStruct(shape, F32) for shape, _ in outs],
        in_specs=[pl.BlockSpec(memory_space=space) for space in ins],
        out_specs=[pl.BlockSpec(memory_space=space) for _, space in outs],
        scratch_shapes=[VMEM(shape, F32) for shape in scratch]
        + ([pltpu.SemaphoreType.DMA(sems)] if sems else [])
        + list(more),
        compiler_params=pltpu.CompilerParams(vmem_limit_bytes=limit << 20),
        cost_estimate=pl.CostEstimate(
            flops=10**7, bytes_accessed=10**7, transcendentals=0
        ),
    )


def shards(
    east_wind, equator_wind, pressure, moisture, albedo, courant, sun_angles, absorption, solar_weights
):
    east, flow, press, moist = east_wind[0], equator_wind[0], pressure[0], moisture[0]
    levels, rows, cols = east.shape
    n_tiles = lax.axis_size("tile")
    half_cols = cols // 4
    swap = [(0, 1), (1, 0)]

    def both_ways(pairs):
        return [pair for a, b in pairs for pair in ((a, b), (b, a))]

    mates = both_ways((t, t + 1) for t in range(0, n_tiles, 2))
    fars = both_ways(
        [
            (g * n_tiles + t, g * n_tiles + t + 1)
            for g in range(2)
            for t in range(1, n_tiles - 1, 2)
        ]
        + [(n_tiles - 1, 2 * n_tiles - 1)]
    )

    field = (levels, rows, cols)
    coarse = (9, 8, half_cols)
    staged = (rows, LANES, LANES)
    series = (2 * SUB, LANES, LANES)
    heat = (8, 8, half_cols)

    keep, send, east, flow, press, half = call(
        prepare_kernel,
        [HBM] * 6,
        [(coarse, VMEM)] * 2 + [(staged, VMEM)] * 3 + [((8, LANES), VMEM)],
        [field, albedo.shape[1:], field, field, field, staged],
        (5, 4),
        [SMEM(courant.shape, F32)],
    )(
        *(
            pltpu.with_memory_space_constraint(x, HBM)
            for x in (courant, moist, albedo[0], east, flow, press)
        )
    )
    other = lax.ppermute(send, "group", swap)

    low, high, mate, far = call(
        alone_kernel,
        [VMEM] * 4,
        [(series, VMEM)] * 4,
        [(rows + 2 * OFF, LANES, LANES)] * 3,
    )(half, east, flow, press)
    from_far = lax.ppermute(far, ("group", "tile"), fars)
    from_mate = lax.ppermute(mate, "tile", mates)

    heat_own, heat_other = call(
        functools.partial(radiate_kernel, n_tiles * rows // 2, cols // 2),
        [SMEM] * 3 + [VMEM] * 2,
        [(heat, VMEM)] * 2,
    )(sun_angles, absorption, solar_weights, keep, other)
    heat_back = lax.ppermute(heat_other, "group", swap)

    east, flow, press = call(
        functools.partial(joined_kernel, n_tiles),
        [VMEM] * 8,
        [(field, HBM)] * 2 + [(field, VMEM)],
        [staged] * 4 + [(rows, 8, cols)] + [field] * 2,
        (4,),
    )(half, east, flow, press, low, high, from_mate, from_far)
    (press,) = call(
        spread_kernel, [VMEM] * 3, [(field, HBM)], [field], (8,)
    )(press, heat_own, heat_back)
    return east[None], flow[None], press[None]


def solution(mesh):
    field = P("group", None, "tile", None)
    return jax.shard_map(
        shards,
        mesh=mesh,
        in_specs=(field,) * 4 + (P("group", "tile", None),) + (P(),) * 4,
        out_specs=(field,) * 3,
        check_vma=False,
    )
```

```python
import functools
import math

import jax
import jax.numpy as jnp
from jax import lax
from jax.experimental import pallas as pl
from jax.experimental.pallas import tpu as pltpu
from jax.sharding import PartitionSpec as P


SUB = 6
HEAT_SCALE = 10.0
MU_OFFSET = 0.1
DIFFUSE = 1.66
LOG2E = 1.4426950408889634
LANES = 128
OFF = 8

VMEM = pltpu.VMEM
SMEM = pltpu.SMEM
HBM = pltpu.HBM
F32 = jnp.float32


def lane_iota(dtype=jnp.int32):
    return lax.broadcasted_iota(dtype, (8, LANES), 1)


def sub_iota():
    return lax.broadcasted_iota(jnp.int32, (8, LANES), 0)


def coarsen(moist, albedo, keep, send):
    width = moist.shape[-1]
    half = keep.shape[-1] // LANES
    even_row = sub_iota() % 2 == 0
    even_lane = lane_iota() % 2 == 0

    def fold(top, bottom):
        return jnp.where(
            even_row, top + pltpu.roll(top, 7, 0), bottom + pltpu.roll(bottom, 1, 0)
        )

    def pack(left, right):
        return jnp.where(
            even_lane,
            left + pltpu.roll(left, LANES - 1, 1),
            right + pltpu.roll(right, 1, 1),
        )

    for level in range(9):
        for block in range(width // (2 * LANES)):
            parts = []
            for side in range(2):
                cols = pl.ds((2 * block + side) * LANES, LANES)
                source = moist if level < 8 else albedo
                index = (level,) if level < 8 else ()
                parts.append((source[(*index, slice(0, 8), cols)], source[(*index, slice(8, 16), cols)]))
            top = pack(parts[0][0], parts[1][0])
            bottom = pack(parts[0][1], parts[1][1])
            value = fold(top, bottom) * 0.25
            if block < half:
                keep[level, :, pl.ds(block * LANES, LANES)] = value
            else:
                send[level, :, pl.ds((block - half) * LANES, LANES)] = value


def turn_in(source, rows, target, scale=None):
    by_row = jnp.swapaxes(source[:, pl.ds(rows, 8), :], 0, 1)
    for row in range(8):
        blocks = [by_row[row][:, b * LANES : (b + 1) * LANES] for b in range(16)]
        flat = jnp.concatenate(blocks, axis=0).T
        values = []
        for half in range(2):
            eights = [flat[8 * k : 8 * k + 8] for k in range(half, 16, 2)]
            turned = jnp.swapaxes(jnp.stack(eights), 0, 1)
            values += [turned[i] for i in range(8)]
        if scale is not None:
            values = [scale * v for v in values]
        store_row(target, rows + row, values)


def turn_out(source, rows, target, by_row, scale=None):
    for row in range(rows, rows + 8):
        values = load_row(source, row)
        if scale is not None:
            values = [scale * v for v in values]
        halves = [jnp.swapaxes(jnp.stack(values[h : h + 8]), 0, 1) for h in (0, 8)]
        flat = jnp.concatenate([halves[k % 2][k // 2] for k in range(16)], axis=0)
        blocks = flat.T
        for b in range(16):
            by_row[row, :, pl.ds(b * LANES, LANES)] = blocks[8 * b : 8 * b + 8]
    target[:, pl.ds(rows, 8), :] = jnp.swapaxes(by_row[pl.ds(rows, 8)], 0, 1)


def prepare_kernel(
    courant_in,
    moist_in,
    albedo_in,
    east_in,
    flow_in,
    press_in,
    keep,
    send,
    east_0,
    flow_0,
    press_0,
    half_out,
    moist,
    albedo,
    east,
    flow,
    press,
    sems,
    courant,
):
    fields = [(flow_in, flow), (east_in, east), (press_in, press)]
    copies = {("courant", 0): pltpu.make_async_copy(courant_in, courant, sems.at[0, 0])}
    for n, (source, target) in enumerate(fields):
        for part in range(4):
            some = (pl.ds(part % 2 * 4, 4), pl.ds(part // 2 * 8, 8))
            copies[n, part // 2, part % 2] = pltpu.make_async_copy(
                source.at[some], target.at[some], sems.at[n + 1, part]
            )
    for part in range(4):
        some = pl.ds(2 * part, 2)
        copies["coarse", part] = pltpu.make_async_copy(
            moist_in.at[some], moist.at[some], sems.at[4, part]
        )
    copies["coarse", 4] = pltpu.make_async_copy(albedo_in, albedo, sems.at[0, 1])
    for copy in copies.values():
        copy.start()

    def wait(*key):
        for name, copy in copies.items():
            if name[: len(key)] == key:
                copy.wait()

    wait("courant")
    half = courant_half(courant)
    half_out[...] = half
    for n, (field, target, scale) in enumerate(
        ((flow, flow_0, None), (east, east_0, None), (press, press_0, half))
    ):
        for part in range(2):
            wait(n, part)
            turn_in(field, 8 * part, target, scale)
    wait("coarse")
    coarsen(moist, albedo, keep, send)


def radiate_kernel(
    rows_total, cols_total, sun, absorption, weights, own, other, heat_own, heat_other
):
    group = lax.axis_index("group")
    tile = lax.axis_index("tile")
    sublane = sub_iota()
    lane = lane_iota()
    row = tile * 8 + sublane // 2 + 4 * (sublane % 2)
    colatitude = 1.0 - (row.astype(F32) + 0.5) / rows_total
    hemisphere = 2.0 * group.astype(F32) - 1.0
    latitude = hemisphere * (0.5 * math.pi) * colatitude
    declination = 0.41 * jnp.sin(jnp.full((8, LANES), sun[0], F32))
    sine = jnp.sin(latitude) * jnp.sin(declination)
    cosine = jnp.cos(latitude) * jnp.cos(declination)
    n_g = absorption.shape[0]

    for block in range(own.shape[-1] // LANES):
        cols = pl.ds(block * LANES, LANES)
        column = block * LANES + lane // 2 + 64 * (lane % 2)
        longitude = 2.0 * math.pi * (column.astype(F32) + 0.5) / cols_total
        mu = sine + cosine * jnp.cos(longitude - sun[1])
        lit = mu > 0.0
        sunlit = jnp.abs(mu)
        slant = 1.0 / (sunlit + MU_OFFSET)
        depth = [jnp.zeros((8, LANES), F32)]
        for level in range(8):
            layer = jnp.where(lit, own[level, :, cols], other[level, :, cols])
            depth.append(depth[-1] + layer)
        surface = jnp.where(lit, own[8, :, cols], other[8, :, cols])
        total = depth[8]
        direct = total * slant
        paths = [depth[j] * slant for j in range(1, 9)]
        paths += [direct + DIFFUSE * (total - depth[j]) for j in range(8)]

        def body(g, carry):
            rate = absorption[g] * (-LOG2E)
            weight = weights[g]
            sums, whole = carry[:-1], carry[-1]
            sums = tuple(a + weight * jnp.exp2(rate * p) for a, p in zip(sums, paths))
            return sums + (whole + weight,)

        zero = jnp.zeros((8, LANES), F32)
        sums = lax.fori_loop(0, n_g, body, (zero,) * 17, unroll=32)
        down = (sums[16],) + sums[:8]
        up = sums[8:16] + (sums[7],)
        scale = sunlit * (HEAT_SCALE / n_g)
        net = [scale * (down[j] - surface * up[j]) for j in range(9)]
        for level in range(8):
            heat = net[level] - net[level + 1]
            heat_own[level, :, cols] = jnp.where(lit, heat, 0.0)
            heat_other[level, :, cols] = jnp.where(lit, 0.0, heat)


def courant_half(courant):
    level = lane_iota() % 8
    value = jnp.full((8, LANES), courant[7], F32)
    for index in range(7):
        value = jnp.where(level == index, courant[index], value)
    return 0.5 * value


def load_row(ref, row):
    return [ref[row, pl.ds(8 * i, 8), :] for i in range(16)]


def store_row(ref, row, values):
    for i, value in enumerate(values):
        if value is not None:
            ref[row, pl.ds(8 * i, 8), :] = value


def past_end(first):
    up = pltpu.roll(first, 7, 0)
    return jnp.where(sub_iota() == 7, pltpu.roll(up, LANES - 8, 1), up)


def before_start(last):
    down = pltpu.roll(last, 1, 0)
    return jnp.where(sub_iota() == 0, pltpu.roll(down, 8, 1), down)


def plus(values, others, sign=1.0):
    if others is None:
        return values
    if values is None:
        return others if sign > 0 else [-o for o in others]
    if sign > 0:
        return [v + o for v, o in zip(values, others)]
    return [v - o for v, o in zip(values, others)]


class Rows:
    def __init__(self, ref, first, rows=()):
        self.ref, self.first, self.known = ref, first, dict.fromkeys(rows)

    def get(self, row):
        if row not in self.known:
            return None
        if self.known[row] is not None:
            return self.known[row]
        return load_row(self.ref, row - self.first)

    def put(self, row, values):
        store_row(self.ref, row - self.first, values)
        self.known[row] = None


def substep(old, new, press_rows, flow_rows, east_rows, rate):
    east, flow, press = old
    new_east, new_flow, new_press = new
    every = sorted(set(press_rows) | {r + 1 for r in flow_rows})
    waiting = []

    def ends():
        row, before, after, pressures, winds = waiting.pop(0)
        low, high = pressures[0] - before, after - pressures[1]
        if winds is not None:
            low, high = winds[0] - low, winds[1] - high
        else:
            low, high = -low, -high
        new_east.put(row, [low] + [None] * 14 + [high])

    for row in every:
        if row in press_rows:
            change = plus(flow.get(row + 1), flow.get(row - 1), -1.0)
            winds = east.get(row)
            if winds is not None:
                ahead = winds[1:] + [past_end(winds[0])]
                behind = [before_start(winds[15])] + winds[:-1]
                change = plus([a - b for a, b in zip(ahead, behind)], change)
            change = [rate * c for c in change]
            here = plus(press.get(row), change, -1.0)
            new_press.put(row, here)
            if row in east_rows:
                slope = [here[i + 1] - here[i - 1] for i in range(1, 15)]
                inside = plus(winds and winds[1:15], slope, -1.0)
                new_east.put(row, [None] + inside + [None])
                waiting.append(
                    (
                        row,
                        before_start(here[15]),
                        past_end(here[0]),
                        (here[1], here[14]),
                        winds and (winds[0], winds[15]),
                    )
                )
        if row - 1 in flow_rows:
            slope = plus(new_press.get(row), new_press.get(row - 2), -1.0)
            new_flow.put(row - 1, plus(flow.get(row - 1), slope, -1.0))
        if len(waiting) > 2:
            ends()
    while waiting:
        ends()


def spans(*pairs):
    return [row for low, high in pairs for row in range(low, high + 1)]


PRESS_SPANS = [
    spans((-1, 16)),
    spans((-3, 18)),
    spans((-5, 6), (9, 20)),
    spans((-5, 4), (11, 20)),
    spans((-3, 2), (13, 18)),
    spans((-1, 0), (15, 16)),
]
EAST_SPANS = [
    spans((-1, 16)),
    spans((-3, 6), (9, 18)),
    spans((-5, 4), (11, 20)),
    spans((-3, 2), (13, 18)),
    spans((-1, 0), (15, 16)),
    [],
]
FLOW_SPANS = [
    spans((-2, 17)),
    spans((-4, 19)),
    spans((-6, 5), (10, 21)),
    spans((-4, 3), (12, 19)),
    spans((-2, 1), (14, 17)),
    [],
]


def alone_kernel(
    half, east_0, flow_0, press_0, low_out, high_out, mate, far, east, flow, press
):
    even = lax.axis_index("tile") % 2 == 0
    rate = half[...] * half[...]
    inner = range(16)

    def record(slot, rows):
        low, first, last, high = [rows.get(r) for r in (-1, 0, 15, 16)]
        zero = [jnp.zeros((8, LANES), F32)] * 16
        store_row(low_out, slot, low or zero)
        store_row(high_out, slot, high or zero)

        @pl.when(even)
        def _():
            store_row(mate, slot, last)
            store_row(far, slot, first)

        @pl.when(jnp.logical_not(even))
        def _():
            store_row(mate, slot, first)
            store_row(far, slot, last)

    state = [Rows(ref, 0, inner) for ref in (east_0, flow_0, press_0)]
    work = [Rows(ref, -OFF) for ref in (east, flow, press)]
    for step in range(SUB):
        record(step, state[1])
        substep(
            state, work, PRESS_SPANS[step], FLOW_SPANS[step], EAST_SPANS[step], rate
        )
        state = work
        record(SUB + step, state[2])


def joined_kernel(
    n_tiles,
    half,
    east_0,
    flow_0,
    press_0,
    low_own,
    high_own,
    from_mate,
    from_far,
    east_out,
    flow_out,
    press_out,
    east,
    flow,
    press,
    by_row,
    ready_east,
    ready_flow,
    sems,
):
    tile = lax.axis_index("tile")
    even = tile % 2 == 0
    rate = half[...] * half[...]
    inner = range(16)
    keep_low = jnp.where(tile == 0, 0.0, 1.0)
    turn = jnp.where(tile == n_tiles - 1, -1.0, 1.0)

    def border(slot, rows, sign):
        mate, far = load_row(from_mate, slot), load_row(from_far, slot)
        own_low, own_high = load_row(low_own, slot), load_row(high_own, slot)
        rows.known[-1] = [
            keep_low * o + jnp.where(even, f, m) for o, m, f in zip(own_low, mate, far)
        ]
        rows.known[16] = [
            o + sign * jnp.where(even, m, f) for o, m, f in zip(own_high, mate, far)
        ]

    state = [Rows(ref, 0, inner) for ref in (east_0, flow_0, press_0)]
    work = [Rows(ref, 0) for ref in (east, flow, press)]
    for step in range(SUB):
        border(step, state[1], turn)
        border(SUB + step, work[2], 1.0)
        substep(state, work, inner, inner, inner, rate)
        state = work
    copies = []
    for field, ready, out in (
        (flow, ready_flow, flow_out),
        (east, ready_east, east_out),
    ):
        for rows in (0, 8):
            turn_out(field, rows, ready, by_row)
            some = pl.ds(rows, 8)
            copies.append(
                pltpu.make_async_copy(
                    ready.at[:, some], out.at[:, some], sems.at[len(copies)]
                )
            )
            copies[-1].start()
    for rows in (0, 8):
        turn_out(press, rows, press_out, by_row, 1.0 / half[...])
    for copy in copies:
        copy.wait()


def spread_kernel(press, heat_own, heat_back, out, ready, sems):
    even_lane = lane_iota() % 2 == 0
    even_row = sub_iota() % 2 == 0
    blocks = heat_own.shape[-1] // LANES
    copies = []
    for level in range(8):
        for block in range(2 * blocks):
            part = heat_own if block < blocks else heat_back
            value = part[level, :, pl.ds(block % blocks * LANES, LANES)]
            left = jnp.where(even_lane, value, pltpu.roll(value, 1, 1))
            right = jnp.where(even_lane, pltpu.roll(value, LANES - 1, 1), value)
            for side, heat in enumerate((left, right)):
                cols = pl.ds((2 * block + side) * LANES, LANES)
                top = jnp.where(even_row, heat, pltpu.roll(heat, 1, 0))
                bottom = jnp.where(even_row, pltpu.roll(heat, 7, 0), heat)
                ready[level, 0:8, cols] = press[level, 0:8, cols] + top
                ready[level, 8:16, cols] = press[level, 8:16, cols] + bottom
        copies.append(
            pltpu.make_async_copy(ready.at[level], out.at[level], sems.at[level])
        )
        copies[-1].start()
    for copy in copies:
        copy.wait()


def call(kernel, ins, outs, scratch=(), sems=None, more=(), limit=16):
    return pl.pallas_call(
        kernel,
        out_shape=[jax.ShapeDtypeStruct(shape, F32) for shape, _ in outs],
        in_specs=[pl.BlockSpec(memory_space=space) for space in ins],
        out_specs=[pl.BlockSpec(memory_space=space) for _, space in outs],
        scratch_shapes=[VMEM(shape, F32) for shape in scratch]
        + ([pltpu.SemaphoreType.DMA(sems)] if sems else [])
        + list(more),
        compiler_params=pltpu.CompilerParams(vmem_limit_bytes=limit << 20),
        cost_estimate=pl.CostEstimate(
            flops=10**7, bytes_accessed=10**7, transcendentals=0
        ),
    )


def shards(
    east_wind, equator_wind, pressure, moisture, albedo, courant, sun_angles, absorption, solar_weights
):
    east, flow, press, moist = east_wind[0], equator_wind[0], pressure[0], moisture[0]
    levels, rows, cols = east.shape
    n_tiles = lax.axis_size("tile")
    half_cols = cols // 4
    swap = [(0, 1), (1, 0)]

    def both_ways(pairs):
        return [pair for a, b in pairs for pair in ((a, b), (b, a))]

    mates = both_ways((t, t + 1) for t in range(0, n_tiles, 2))
    fars = both_ways(
        [
            (g * n_tiles + t, g * n_tiles + t + 1)
            for g in range(2)
            for t in range(1, n_tiles - 1, 2)
        ]
        + [(n_tiles - 1, 2 * n_tiles - 1)]
    )

    field = (levels, rows, cols)
    coarse = (9, 8, half_cols)
    staged = (rows, LANES, LANES)
    series = (2 * SUB, LANES, LANES)
    heat = (8, 8, half_cols)

    keep, send, east, flow, press, half = call(
        prepare_kernel,
        [HBM] * 6,
        [(coarse, VMEM)] * 2 + [(staged, VMEM)] * 3 + [((8, LANES), VMEM)],
        [field, albedo.shape[1:], field, field, field],
        (5, 4),
        [SMEM(courant.shape, F32)],
    )(
        *(
            pltpu.with_memory_space_constraint(x, HBM)
            for x in (courant, moist, albedo[0], east, flow, press)
        )
    )
    other = lax.ppermute(send, "group", swap)

    low, high, mate, far = call(
        alone_kernel,
        [VMEM] * 4,
        [(series, VMEM)] * 4,
        [(rows + 2 * OFF, LANES, LANES)] * 3,
    )(half, east, flow, press)
    from_far = lax.ppermute(far, ("group", "tile"), fars)
    from_mate = lax.ppermute(mate, "tile", mates)

    heat_own, heat_other = call(
        functools.partial(radiate_kernel, n_tiles * rows // 2, cols // 2),
        [SMEM] * 3 + [VMEM] * 2,
        [(heat, VMEM)] * 2,
    )(sun_angles, absorption, solar_weights, keep, other)
    heat_back = lax.ppermute(heat_other, "group", swap)

    east, flow, press = call(
        functools.partial(joined_kernel, n_tiles),
        [VMEM] * 8,
        [(field, HBM)] * 2 + [(field, VMEM)],
        [staged] * 3 + [(rows, 8, cols)] + [field] * 2,
        (4,),
    )(half, east, flow, press, low, high, from_mate, from_far)
    (press,) = call(
        spread_kernel, [VMEM] * 3, [(field, HBM)], [field], (8,)
    )(press, heat_own, heat_back)
    return east[None], flow[None], press[None]


def solution(mesh):
    field = P("group", None, "tile", None)
    return jax.shard_map(
        shards,
        mesh=mesh,
        in_specs=(field,) * 4 + (P("group", "tile", None),) + (P(),) * 4,
        out_specs=(field,) * 3,
        check_vma=False,
    )
```

```python
import functools
import math

import jax
import jax.numpy as jnp
from jax import lax
from jax.experimental import pallas as pl
from jax.experimental.pallas import tpu as pltpu
from jax.sharding import PartitionSpec as P


SUB = 6
HEAT_SCALE = 10.0
MU_OFFSET = 0.1
DIFFUSE = 1.66
LOG2E = 1.4426950408889634
LANES = 128
OFF = 8

VMEM = pltpu.VMEM
SMEM = pltpu.SMEM
HBM = pltpu.HBM
F32 = jnp.float32


def lane_iota(dtype=jnp.int32):
    return lax.broadcasted_iota(dtype, (8, LANES), 1)


def sub_iota():
    return lax.broadcasted_iota(jnp.int32, (8, LANES), 0)


def coarsen(moist, albedo, keep, send):
    width = moist.shape[-1]
    half = keep.shape[-1] // LANES
    even_row = sub_iota() % 2 == 0
    even_lane = lane_iota() % 2 == 0

    def fold(top, bottom):
        return jnp.where(
            even_row, top + pltpu.roll(top, 7, 0), bottom + pltpu.roll(bottom, 1, 0)
        )

    def pack(left, right):
        return jnp.where(
            even_lane,
            left + pltpu.roll(left, LANES - 1, 1),
            right + pltpu.roll(right, 1, 1),
        )

    for level in range(9):
        for block in range(width // (2 * LANES)):
            parts = []
            for side in range(2):
                cols = pl.ds((2 * block + side) * LANES, LANES)
                source = moist if level < 8 else albedo
                index = (level,) if level < 8 else ()
                parts.append((source[(*index, slice(0, 8), cols)], source[(*index, slice(8, 16), cols)]))
            top = pack(parts[0][0], parts[1][0])
            bottom = pack(parts[0][1], parts[1][1])
            value = fold(top, bottom) * 0.25
            if block < half:
                keep[level, :, pl.ds(block * LANES, LANES)] = value
            else:
                send[level, :, pl.ds((block - half) * LANES, LANES)] = value


def turn_in(source, rows, target, scale=None):
    by_row = jnp.swapaxes(source[:, pl.ds(rows, 8), :], 0, 1)
    for row in range(8):
        blocks = [by_row[row][:, b * LANES : (b + 1) * LANES] for b in range(16)]
        flat = jnp.concatenate(blocks, axis=0).T
        values = []
        for half in range(2):
            eights = [flat[8 * k : 8 * k + 8] for k in range(half, 16, 2)]
            turned = jnp.swapaxes(jnp.stack(eights), 0, 1)
            values += [turned[i] for i in range(8)]
        if scale is not None:
            values = [scale * v for v in values]
        store_row(target, rows + row, values)


def turn_out(source, rows, target, by_row, scale=None):
    for row in range(rows, rows + 8):
        values = load_row(source, row)
        if scale is not None:
            values = [scale * v for v in values]
        halves = [jnp.swapaxes(jnp.stack(values[h : h + 8]), 0, 1) for h in (0, 8)]
        flat = jnp.concatenate([halves[k % 2][k // 2] for k in range(16)], axis=0)
        blocks = flat.T
        for b in range(16):
            by_row[row, :, pl.ds(b * LANES, LANES)] = blocks[8 * b : 8 * b + 8]
    target[:, pl.ds(rows, 8), :] = jnp.swapaxes(by_row[pl.ds(rows, 8)], 0, 1)


def prepare_kernel(
    courant_in,
    sun_in,
    absorption_in,
    weights_in,
    moist_in,
    albedo_in,
    east_in,
    flow_in,
    press_in,
    keep,
    send,
    east_0,
    flow_0,
    press_0,
    half_out,
    sun_out,
    absorption,
    weights,
    moist,
    albedo,
    east,
    flow,
    press,
    sems,
    courant,
    sun,
):
    fields = [(flow_in, flow), (east_in, east), (press_in, press)]
    copies = {
        ("small", 0): pltpu.make_async_copy(courant_in, courant, sems.at[0, 0]),
        ("small", 1): pltpu.make_async_copy(sun_in, sun, sems.at[0, 2]),
    }
    for n, (source, target) in enumerate(fields):
        for part in range(4):
            some = (pl.ds(part % 2 * 4, 4), pl.ds(part // 2 * 8, 8))
            copies[n, part // 2, part % 2] = pltpu.make_async_copy(
                source.at[some], target.at[some], sems.at[n + 1, part]
            )
    for part in range(4):
        some = pl.ds(2 * part, 2)
        copies["coarse", part] = pltpu.make_async_copy(
            moist_in.at[some], moist.at[some], sems.at[4, part]
        )
    copies["coarse", 4] = pltpu.make_async_copy(albedo_in, albedo, sems.at[0, 1])
    copies["rates", 0] = pltpu.make_async_copy(absorption_in, absorption, sems.at[0, 3])
    copies["rates", 1] = pltpu.make_async_copy(weights_in, weights, sems.at[5, 0])
    for copy in copies.values():
        copy.start()

    def wait(*key):
        for name, copy in copies.items():
            if name[: len(key)] == key:
                copy.wait()

    wait("small")
    half = courant_half(courant)
    half_out[...] = half
    for index in range(2):
        sun_out[index] = jnp.full((8, LANES), sun[index], F32)
    for n, (field, target, scale) in enumerate(
        ((flow, flow_0, None), (east, east_0, None), (press, press_0, half))
    ):
        for part in range(2):
            wait(n, part)
            turn_in(field, 8 * part, target, scale)
    wait("coarse")
    coarsen(moist, albedo, keep, send)
    wait("rates")


def radiate_kernel(
    rows_total, cols_total, absorption, weights, sun, own, other, heat_own, heat_other
):
    group = lax.axis_index("group")
    tile = lax.axis_index("tile")
    sublane = sub_iota()
    lane = lane_iota()
    row = tile * 8 + sublane // 2 + 4 * (sublane % 2)
    colatitude = 1.0 - (row.astype(F32) + 0.5) / rows_total
    hemisphere = 2.0 * group.astype(F32) - 1.0
    latitude = hemisphere * (0.5 * math.pi) * colatitude
    declination = 0.41 * jnp.sin(sun[0])
    sine = jnp.sin(latitude) * jnp.sin(declination)
    cosine = jnp.cos(latitude) * jnp.cos(declination)
    n_g = absorption.shape[0]

    for block in range(own.shape[-1] // LANES):
        cols = pl.ds(block * LANES, LANES)
        column = block * LANES + lane // 2 + 64 * (lane % 2)
        longitude = 2.0 * math.pi * (column.astype(F32) + 0.5) / cols_total
        mu = sine + cosine * jnp.cos(longitude - sun[1])
        lit = mu > 0.0
        sunlit = jnp.abs(mu)
        slant = 1.0 / (sunlit + MU_OFFSET)
        depth = [jnp.zeros((8, LANES), F32)]
        for level in range(8):
            layer = jnp.where(lit, own[level, :, cols], other[level, :, cols])
            depth.append(depth[-1] + layer)
        surface = jnp.where(lit, own[8, :, cols], other[8, :, cols])
        total = depth[8]
        direct = total * slant
        paths = [depth[j] * slant for j in range(1, 9)]
        paths += [direct + DIFFUSE * (total - depth[j]) for j in range(8)]

        def body(g, carry):
            rate = absorption[g] * (-LOG2E)
            weight = weights[g]
            sums, whole = carry[:-1], carry[-1]
            sums = tuple(a + weight * jnp.exp2(rate * p) for a, p in zip(sums, paths))
            return sums + (whole + weight,)

        zero = jnp.zeros((8, LANES), F32)
        sums = lax.fori_loop(0, n_g, body, (zero,) * 17, unroll=32)
        down = (sums[16],) + sums[:8]
        up = sums[8:16] + (sums[7],)
        scale = sunlit * (HEAT_SCALE / n_g)
        net = [scale * (down[j] - surface * up[j]) for j in range(9)]
        for level in range(8):
            heat = net[level] - net[level + 1]
            heat_own[level, :, cols] = jnp.where(lit, heat, 0.0)
            heat_other[level, :, cols] = jnp.where(lit, 0.0, heat)


def courant_half(courant):
    level = lane_iota() % 8
    value = jnp.full((8, LANES), courant[7], F32)
    for index in range(7):
        value = jnp.where(level == index, courant[index], value)
    return 0.5 * value


def load_row(ref, row):
    return [ref[row, pl.ds(8 * i, 8), :] for i in range(16)]


def store_row(ref, row, values):
    for i, value in enumerate(values):
        if value is not None:
            ref[row, pl.ds(8 * i, 8), :] = value


def past_end(first):
    up = pltpu.roll(first, 7, 0)
    return jnp.where(sub_iota() == 7, pltpu.roll(up, LANES - 8, 1), up)


def before_start(last):
    down = pltpu.roll(last, 1, 0)
    return jnp.where(sub_iota() == 0, pltpu.roll(down, 8, 1), down)


def plus(values, others, sign=1.0):
    if others is None:
        return values
    if values is None:
        return others if sign > 0 else [-o for o in others]
    if sign > 0:
        return [v + o for v, o in zip(values, others)]
    return [v - o for v, o in zip(values, others)]


class Rows:
    def __init__(self, ref, first, rows=()):
        self.ref, self.first, self.known = ref, first, dict.fromkeys(rows)

    def get(self, row):
        if row not in self.known:
            return None
        if self.known[row] is not None:
            return self.known[row]
        return load_row(self.ref, row - self.first)

    def put(self, row, values):
        store_row(self.ref, row - self.first, values)
        self.known[row] = None


def substep(old, new, press_rows, flow_rows, east_rows, rate):
    east, flow, press = old
    new_east, new_flow, new_press = new
    every = sorted(set(press_rows) | {r + 1 for r in flow_rows})
    waiting = []

    def ends():
        row, before, after, pressures, winds = waiting.pop(0)
        low, high = pressures[0] - before, after - pressures[1]
        if winds is not None:
            low, high = winds[0] - low, winds[1] - high
        else:
            low, high = -low, -high
        new_east.put(row, [low] + [None] * 14 + [high])

    for row in every:
        if row in press_rows:
            change = plus(flow.get(row + 1), flow.get(row - 1), -1.0)
            winds = east.get(row)
            if winds is not None:
                ahead = winds[1:] + [past_end(winds[0])]
                behind = [before_start(winds[15])] + winds[:-1]
                change = plus([a - b for a, b in zip(ahead, behind)], change)
            change = [rate * c for c in change]
            here = plus(press.get(row), change, -1.0)
            new_press.put(row, here)
            if row in east_rows:
                slope = [here[i + 1] - here[i - 1] for i in range(1, 15)]
                inside = plus(winds and winds[1:15], slope, -1.0)
                new_east.put(row, [None] + inside + [None])
                waiting.append(
                    (
                        row,
                        before_start(here[15]),
                        past_end(here[0]),
                        (here[1], here[14]),
                        winds and (winds[0], winds[15]),
                    )
                )
        if row - 1 in flow_rows:
            slope = plus(new_press.get(row), new_press.get(row - 2), -1.0)
            new_flow.put(row - 1, plus(flow.get(row - 1), slope, -1.0))
        if len(waiting) > 2:
            ends()
    while waiting:
        ends()


def spans(*pairs):
    return [row for low, high in pairs for row in range(low, high + 1)]


PRESS_SPANS = [
    spans((-1, 16)),
    spans((-3, 18)),
    spans((-5, 6), (9, 20)),
    spans((-5, 4), (11, 20)),
    spans((-3, 2), (13, 18)),
    spans((-1, 0), (15, 16)),
]
EAST_SPANS = [
    spans((-1, 16)),
    spans((-3, 6), (9, 18)),
    spans((-5, 4), (11, 20)),
    spans((-3, 2), (13, 18)),
    spans((-1, 0), (15, 16)),
    [],
]
FLOW_SPANS = [
    spans((-2, 17)),
    spans((-4, 19)),
    spans((-6, 5), (10, 21)),
    spans((-4, 3), (12, 19)),
    spans((-2, 1), (14, 17)),
    [],
]


def alone_kernel(
    half, east_0, flow_0, press_0, low_out, high_out, mate, far, east, flow, press
):
    even = lax.axis_index("tile") % 2 == 0
    rate = half[...] * half[...]
    inner = range(16)

    def record(slot, rows):
        low, first, last, high = [rows.get(r) for r in (-1, 0, 15, 16)]
        zero = [jnp.zeros((8, LANES), F32)] * 16
        store_row(low_out, slot, low or zero)
        store_row(high_out, slot, high or zero)

        @pl.when(even)
        def _():
            store_row(mate, slot, last)
            store_row(far, slot, first)

        @pl.when(jnp.logical_not(even))
        def _():
            store_row(mate, slot, first)
            store_row(far, slot, last)

    state = [Rows(ref, 0, inner) for ref in (east_0, flow_0, press_0)]
    work = [Rows(ref, -OFF) for ref in (east, flow, press)]
    for step in range(SUB):
        record(step, state[1])
        substep(
            state, work, PRESS_SPANS[step], FLOW_SPANS[step], EAST_SPANS[step], rate
        )
        state = work
        record(SUB + step, state[2])


def joined_kernel(
    n_tiles,
    half,
    east_0,
    flow_0,
    press_0,
    low_own,
    high_own,
    from_mate,
    from_far,
    east_out,
    flow_out,
    press_out,
    east,
    flow,
    press,
    by_row,
    ready_east,
    ready_flow,
    sems,
):
    tile = lax.axis_index("tile")
    even = tile % 2 == 0
    rate = half[...] * half[...]
    inner = range(16)
    keep_low = jnp.where(tile == 0, 0.0, 1.0)
    turn = jnp.where(tile == n_tiles - 1, -1.0, 1.0)

    def border(slot, rows, sign):
        mate, far = load_row(from_mate, slot), load_row(from_far, slot)
        own_low, own_high = load_row(low_own, slot), load_row(high_own, slot)
        rows.known[-1] = [
            keep_low * o + jnp.where(even, f, m) for o, m, f in zip(own_low, mate, far)
        ]
        rows.known[16] = [
            o + sign * jnp.where(even, m, f) for o, m, f in zip(own_high, mate, far)
        ]

    state = [Rows(ref, 0, inner) for ref in (east_0, flow_0, press_0)]
    work = [Rows(ref, 0) for ref in (east, flow, press)]
    for step in range(SUB):
        border(step, state[1], turn)
        border(SUB + step, work[2], 1.0)
        substep(state, work, inner, inner, inner, rate)
        state = work
    copies = []
    for field, ready, out in (
        (flow, ready_flow, flow_out),
        (east, ready_east, east_out),
    ):
        for rows in (0, 8):
            turn_out(field, rows, ready, by_row)
            some = pl.ds(rows, 8)
            copies.append(
                pltpu.make_async_copy(
                    ready.at[:, some], out.at[:, some], sems.at[len(copies)]
                )
            )
            copies[-1].start()
    for rows in (0, 8):
        turn_out(press, rows, press_out, by_row, 1.0 / half[...])
    for copy in copies:
        copy.wait()


def spread_kernel(press, heat_own, heat_back, out, ready, sems):
    even_lane = lane_iota() % 2 == 0
    even_row = sub_iota() % 2 == 0
    blocks = heat_own.shape[-1] // LANES
    copies = []
    for level in range(8):
        for block in range(2 * blocks):
            part = heat_own if block < blocks else heat_back
            value = part[level, :, pl.ds(block % blocks * LANES, LANES)]
            left = jnp.where(even_lane, value, pltpu.roll(value, 1, 1))
            right = jnp.where(even_lane, pltpu.roll(value, LANES - 1, 1), value)
            for side, heat in enumerate((left, right)):
                cols = pl.ds((2 * block + side) * LANES, LANES)
                top = jnp.where(even_row, heat, pltpu.roll(heat, 1, 0))
                bottom = jnp.where(even_row, pltpu.roll(heat, 7, 0), heat)
                ready[level, 0:8, cols] = press[level, 0:8, cols] + top
                ready[level, 8:16, cols] = press[level, 8:16, cols] + bottom
        copies.append(
            pltpu.make_async_copy(ready.at[level], out.at[level], sems.at[level])
        )
        copies[-1].start()
    for copy in copies:
        copy.wait()


def call(kernel, ins, outs, scratch=(), sems=None, more=(), limit=16):
    return pl.pallas_call(
        kernel,
        out_shape=[jax.ShapeDtypeStruct(shape, F32) for shape, _ in outs],
        in_specs=[pl.BlockSpec(memory_space=space) for space in ins],
        out_specs=[pl.BlockSpec(memory_space=space) for _, space in outs],
        scratch_shapes=[VMEM(shape, F32) for shape in scratch]
        + ([pltpu.SemaphoreType.DMA(sems)] if sems else [])
        + list(more),
        compiler_params=pltpu.CompilerParams(vmem_limit_bytes=limit << 20),
        cost_estimate=pl.CostEstimate(
            flops=10**7, bytes_accessed=10**7, transcendentals=0
        ),
    )


def shards(
    east_wind, equator_wind, pressure, moisture, albedo, courant, sun_angles, absorption, solar_weights
):
    east, flow, press, moist = east_wind[0], equator_wind[0], pressure[0], moisture[0]
    levels, rows, cols = east.shape
    n_tiles = lax.axis_size("tile")
    half_cols = cols // 4
    swap = [(0, 1), (1, 0)]

    def both_ways(pairs):
        return [pair for a, b in pairs for pair in ((a, b), (b, a))]

    mates = both_ways((t, t + 1) for t in range(0, n_tiles, 2))
    fars = both_ways(
        [
            (g * n_tiles + t, g * n_tiles + t + 1)
            for g in range(2)
            for t in range(1, n_tiles - 1, 2)
        ]
        + [(n_tiles - 1, 2 * n_tiles - 1)]
    )

    field = (levels, rows, cols)
    coarse = (9, 8, half_cols)
    staged = (rows, LANES, LANES)
    series = (2 * SUB, LANES, LANES)
    heat = (8, 8, half_cols)

    keep, send, east, flow, press, half, sun, absorb, weights = call(
        prepare_kernel,
        [HBM] * 9,
        [(coarse, VMEM)] * 2
        + [(staged, VMEM)] * 3
        + [((8, LANES), VMEM), ((2, 8, LANES), VMEM)]
        + [(absorption.shape, VMEM)] * 2,
        [field, albedo.shape[1:], field, field, field],
        (6, 4),
        [SMEM(courant.shape, F32), SMEM(sun_angles.shape, F32)],
    )(
        *(
            pltpu.with_memory_space_constraint(x, HBM)
            for x in (
                courant,
                sun_angles,
                absorption,
                solar_weights,
                moist,
                albedo[0],
                east,
                flow,
                press,
            )
        )
    )
    other = lax.ppermute(send, "group", swap)

    low, high, mate, far = call(
        alone_kernel,
        [VMEM] * 4,
        [(series, VMEM)] * 4,
        [(rows + 2 * OFF, LANES, LANES)] * 3,
    )(half, east, flow, press)
    from_far = lax.ppermute(far, ("group", "tile"), fars)
    from_mate = lax.ppermute(mate, "tile", mates)

    heat_own, heat_other = call(
        functools.partial(radiate_kernel, n_tiles * rows // 2, cols // 2),
        [SMEM] * 2 + [VMEM] * 3,
        [(heat, VMEM)] * 2,
    )(absorb, weights, sun, keep, other)
    heat_back = lax.ppermute(heat_other, "group", swap)

    east, flow, press = call(
        functools.partial(joined_kernel, n_tiles),
        [VMEM] * 8,
        [(field, HBM)] * 2 + [(field, VMEM)],
        [staged] * 3 + [(rows, 8, cols)] + [field] * 2,
        (4,),
    )(half, east, flow, press, low, high, from_mate, from_far)
    (press,) = call(
        spread_kernel, [VMEM] * 3, [(field, HBM)], [field], (8,)
    )(press, heat_own, heat_back)
    return east[None], flow[None], press[None]


def solution(mesh):
    field = P("group", None, "tile", None)
    return jax.shard_map(
        shards,
        mesh=mesh,
        in_specs=(field,) * 4 + (P("group", "tile", None),) + (P(),) * 4,
        out_specs=(field,) * 3,
        check_vma=False,
    )
```

```python
import functools
import math

import jax
import jax.numpy as jnp
from jax import lax
from jax.experimental import pallas as pl
from jax.experimental.pallas import tpu as pltpu
from jax.sharding import PartitionSpec as P


SUB = 6
HEAT_SCALE = 10.0
MU_OFFSET = 0.1
DIFFUSE = 1.66
LOG2E = 1.4426950408889634
LANES = 128
OFF = 8

VMEM = pltpu.VMEM
SMEM = pltpu.SMEM
HBM = pltpu.HBM
F32 = jnp.float32


def lane_iota(dtype=jnp.int32):
    return lax.broadcasted_iota(dtype, (8, LANES), 1)


def sub_iota():
    return lax.broadcasted_iota(jnp.int32, (8, LANES), 0)


def coarsen(moist, albedo, keep, send):
    width = moist.shape[-1]
    half = keep.shape[-1] // LANES
    even_row = sub_iota() % 2 == 0
    even_lane = lane_iota() % 2 == 0

    def fold(top, bottom):
        return jnp.where(
            even_row, top + pltpu.roll(top, 7, 0), bottom + pltpu.roll(bottom, 1, 0)
        )

    def pack(left, right):
        return jnp.where(
            even_lane,
            left + pltpu.roll(left, LANES - 1, 1),
            right + pltpu.roll(right, 1, 1),
        )

    for level in range(9):
        for block in range(width // (2 * LANES)):
            parts = []
            for side in range(2):
                cols = pl.ds((2 * block + side) * LANES, LANES)
                source = moist if level < 8 else albedo
                index = (level,) if level < 8 else ()
                parts.append((source[(*index, slice(0, 8), cols)], source[(*index, slice(8, 16), cols)]))
            top = pack(parts[0][0], parts[1][0])
            bottom = pack(parts[0][1], parts[1][1])
            value = fold(top, bottom) * 0.25
            if block < half:
                keep[level, :, pl.ds(block * LANES, LANES)] = value
            else:
                send[level, :, pl.ds((block - half) * LANES, LANES)] = value


def turn_in(source, rows, target, scale=None):
    by_row = jnp.swapaxes(source[:, pl.ds(rows, 8), :], 0, 1)
    for row in range(8):
        blocks = [by_row[row][:, b * LANES : (b + 1) * LANES] for b in range(16)]
        flat = jnp.concatenate(blocks, axis=0).T
        values = []
        for half in range(2):
            eights = [flat[8 * k : 8 * k + 8] for k in range(half, 16, 2)]
            turned = jnp.swapaxes(jnp.stack(eights), 0, 1)
            values += [turned[i] for i in range(8)]
        if scale is not None:
            values = [scale * v for v in values]
        store_row(target, rows + row, values)


def turn_out(source, rows, target, by_row, scale=None):
    for row in range(rows, rows + 8):
        values = load_row(source, row)
        if scale is not None:
            values = [scale * v for v in values]
        halves = [jnp.swapaxes(jnp.stack(values[h : h + 8]), 0, 1) for h in (0, 8)]
        flat = jnp.concatenate([halves[k % 2][k // 2] for k in range(16)], axis=0)
        blocks = flat.T
        for b in range(16):
            by_row[row, :, pl.ds(b * LANES, LANES)] = blocks[8 * b : 8 * b + 8]
    target[:, pl.ds(rows, 8), :] = jnp.swapaxes(by_row[pl.ds(rows, 8)], 0, 1)


def prepare_kernel(
    courant_in,
    sun_in,
    absorption_in,
    weights_in,
    moist_in,
    albedo_in,
    east_in,
    flow_in,
    press_in,
    keep,
    send,
    east_0,
    flow_0,
    press_0,
    half_out,
    sun_out,
    absorption,
    weights,
    moist,
    albedo,
    east,
    flow,
    press,
    sems,
    courant,
    sun,
):
    fields = [(flow_in, flow), (east_in, east), (press_in, press)]
    copies = {
        ("small", 0): pltpu.make_async_copy(courant_in, courant, sems.at[0, 0]),
        ("small", 1): pltpu.make_async_copy(sun_in, sun, sems.at[0, 2]),
    }
    for n, (source, target) in enumerate(fields):
        for part in range(4):
            some = (pl.ds(part % 2 * 4, 4), pl.ds(part // 2 * 8, 8))
            copies[n, part // 2, part % 2] = pltpu.make_async_copy(
                source.at[some], target.at[some], sems.at[n + 1, part]
            )
    for part in range(4):
        some = pl.ds(2 * part, 2)
        copies["coarse", part] = pltpu.make_async_copy(
            moist_in.at[some], moist.at[some], sems.at[4, part]
        )
    copies["coarse", 4] = pltpu.make_async_copy(albedo_in, albedo, sems.at[0, 1])
    copies["rates", 0] = pltpu.make_async_copy(absorption_in, absorption, sems.at[0, 3])
    copies["rates", 1] = pltpu.make_async_copy(weights_in, weights, sems.at[5, 0])
    for copy in copies.values():
        copy.start()

    def wait(*key):
        for name, copy in copies.items():
            if name[: len(key)] == key:
                copy.wait()

    wait("small")
    half = courant_half(courant)
    half_out[...] = half
    for index in range(2):
        sun_out[index] = jnp.full((8, LANES), sun[index], F32)
    for n, (field, target, scale) in enumerate(
        ((flow, flow_0, None), (east, east_0, None), (press, press_0, half))
    ):
        for part in range(2):
            wait(n, part)
            turn_in(field, 8 * part, target, scale)
    wait("coarse")
    coarsen(moist, albedo, keep, send)
    wait("rates")


def radiate_kernel(
    rows_total, cols_total, absorption, weights, sun, own, other, heat_own, heat_other
):
    group = lax.axis_index("group")
    tile = lax.axis_index("tile")
    sublane = sub_iota()
    lane = lane_iota()
    row = tile * 8 + sublane // 2 + 4 * (sublane % 2)
    colatitude = 1.0 - (row.astype(F32) + 0.5) / rows_total
    hemisphere = 2.0 * group.astype(F32) - 1.0
    latitude = hemisphere * (0.5 * math.pi) * colatitude
    declination = 0.41 * jnp.sin(sun[0])
    sine = jnp.sin(latitude) * jnp.sin(declination)
    cosine = jnp.cos(latitude) * jnp.cos(declination)
    n_g = absorption.shape[0]

    for block in range(own.shape[-1] // LANES):
        cols = pl.ds(block * LANES, LANES)
        column = block * LANES + lane // 2 + 64 * (lane % 2)
        longitude = 2.0 * math.pi * (column.astype(F32) + 0.5) / cols_total
        mu = sine + cosine * jnp.cos(longitude - sun[1])
        lit = mu > 0.0
        sunlit = jnp.abs(mu)
        slant = 1.0 / (sunlit + MU_OFFSET)
        depth = [jnp.zeros((8, LANES), F32)]
        for level in range(8):
            layer = jnp.where(lit, own[level, :, cols], other[level, :, cols])
            depth.append(depth[-1] + layer)
        surface = jnp.where(lit, own[8, :, cols], other[8, :, cols])
        total = depth[8]
        direct = total * slant
        paths = [depth[j] * slant for j in range(1, 9)]
        paths += [direct + DIFFUSE * (total - depth[j]) for j in range(8)]

        def body(g, carry):
            rate = absorption[g] * (-LOG2E)
            weight = weights[g]
            sums, whole = carry[:-1], carry[-1]
            sums = tuple(a + weight * jnp.exp2(rate * p) for a, p in zip(sums, paths))
            return sums + (whole + weight,)

        zero = jnp.zeros((8, LANES), F32)
        sums = lax.fori_loop(0, n_g, body, (zero,) * 17, unroll=32)
        down = (sums[16],) + sums[:8]
        up = sums[8:16] + (sums[7],)
        scale = sunlit * (HEAT_SCALE / n_g)
        net = [scale * (down[j] - surface * up[j]) for j in range(9)]
        for level in range(8):
            heat = net[level] - net[level + 1]
            heat_own[level, :, cols] = jnp.where(lit, heat, 0.0)
            heat_other[level, :, cols] = jnp.where(lit, 0.0, heat)


def courant_half(courant):
    level = lane_iota() % 8
    value = jnp.full((8, LANES), courant[7], F32)
    for index in range(7):
        value = jnp.where(level == index, courant[index], value)
    return 0.5 * value


def load_row(ref, row):
    return [ref[row, pl.ds(8 * i, 8), :] for i in range(16)]


def store_row(ref, row, values):
    for i, value in enumerate(values):
        if value is not None:
            ref[row, pl.ds(8 * i, 8), :] = value


def past_end(first):
    up = pltpu.roll(first, 7, 0)
    return jnp.where(sub_iota() == 7, pltpu.roll(up, LANES - 8, 1), up)


def before_start(last):
    down = pltpu.roll(last, 1, 0)
    return jnp.where(sub_iota() == 0, pltpu.roll(down, 8, 1), down)


def plus(values, others, sign=1.0):
    if others is None:
        return values
    if values is None:
        return others if sign > 0 else [-o for o in others]
    if sign > 0:
        return [v + o for v, o in zip(values, others)]
    return [v - o for v, o in zip(values, others)]


class Rows:
    def __init__(self, ref, first, rows=()):
        self.ref, self.first, self.known = ref, first, dict.fromkeys(rows)

    def get(self, row):
        if row not in self.known:
            return None
        if self.known[row] is not None:
            return self.known[row]
        return load_row(self.ref, row - self.first)

    def put(self, row, values):
        store_row(self.ref, row - self.first, values)
        self.known[row] = None


def substep(old, new, press_rows, flow_rows, east_rows, rate):
    east, flow, press = old
    new_east, new_flow, new_press = new
    every = sorted(set(press_rows) | {r + 1 for r in flow_rows})
    waiting = []

    def ends():
        row, before, after, pressures, winds = waiting.pop(0)
        low, high = pressures[0] - before, after - pressures[1]
        if winds is not None:
            low, high = winds[0] - low, winds[1] - high
        else:
            low, high = -low, -high
        new_east.put(row, [low] + [None] * 14 + [high])

    for row in every:
        if row in press_rows:
            change = plus(flow.get(row + 1), flow.get(row - 1), -1.0)
            winds = east.get(row)
            if winds is not None:
                ahead = winds[1:] + [past_end(winds[0])]
                behind = [before_start(winds[15])] + winds[:-1]
                change = plus([a - b for a, b in zip(ahead, behind)], change)
            change = [rate * c for c in change]
            here = plus(press.get(row), change, -1.0)
            new_press.put(row, here)
            if row in east_rows:
                slope = [here[i + 1] - here[i - 1] for i in range(1, 15)]
                inside = plus(winds and winds[1:15], slope, -1.0)
                new_east.put(row, [None] + inside + [None])
                waiting.append(
                    (
                        row,
                        before_start(here[15]),
                        past_end(here[0]),
                        (here[1], here[14]),
                        winds and (winds[0], winds[15]),
                    )
                )
        if row - 1 in flow_rows:
            slope = plus(new_press.get(row), new_press.get(row - 2), -1.0)
            new_flow.put(row - 1, plus(flow.get(row - 1), slope, -1.0))
        if len(waiting) > 2:
            ends()
    while waiting:
        ends()


PRESS_SPANS = [(-1, 10), (-3, 8), (-5, 6), (-5, 4), (-3, 2), (-1, 0)]
EAST_SPANS = [(-1, 8), (-3, 6), (-5, 4), (-3, 2), (-1, 0), (0, -1)]
FLOW_SPANS = [(-2, 9), (-4, 7), (-6, 5), (-4, 3), (-2, 1), (0, -1)]


def alone_kernel(
    is_far, half, east_0, flow_0, press_0, own, send, east, flow, press
):
    even = lax.axis_index("tile") % 2 == 0
    rate = half[...] * half[...]

    def run(place):
        def span(pair):
            return sorted(place(row) for row in range(pair[0], pair[1] + 1))

        def record(slot, rows):
            zero = [jnp.zeros((8, LANES), F32)] * 16
            store_row(own, slot, rows.get(place(-1)) or zero)
            store_row(send, slot, rows.get(place(0)))

        state = [Rows(ref, 0, range(16)) for ref in (east_0, flow_0, press_0)]
        work = [Rows(ref, -OFF) for ref in (east, flow, press)]
        for step in range(SUB):
            record(step, state[1])
            spans = [s[step] for s in (PRESS_SPANS, FLOW_SPANS, EAST_SPANS)]
            substep(state, work, *map(span, spans), rate)
            state = work
            record(SUB + step, state[2])

    low = even if is_far else jnp.logical_not(even)
    pl.when(low)(lambda: run(lambda row: row))
    pl.when(jnp.logical_not(low))(lambda: run(lambda row: 15 - row))


def joined_kernel(
    n_tiles,
    half,
    east_0,
    flow_0,
    press_0,
    own_mate,
    own_far,
    from_mate,
    from_far,
    east_out,
    flow_out,
    press_out,
    east,
    flow,
    press,
    by_row,
    ready_east,
    ready_flow,
    sems,
):
    tile = lax.axis_index("tile")
    even = tile % 2 == 0
    rate = half[...] * half[...]
    inner = range(16)
    keep = jnp.where(tile == 0, 0.0, 1.0)
    turn = jnp.where(tile == n_tiles - 1, -1.0, 1.0)

    def border(slot, rows, sign):
        mate = plus(load_row(own_mate, slot), load_row(from_mate, slot))
        far = [
            keep * o + sign * f
            for o, f in zip(load_row(own_far, slot), load_row(from_far, slot))
        ]
        rows.known[-1] = [jnp.where(even, f, m) for m, f in zip(mate, far)]
        rows.known[16] = [jnp.where(even, m, f) for m, f in zip(mate, far)]

    state = [Rows(ref, 0, inner) for ref in (east_0, flow_0, press_0)]
    work = [Rows(ref, 0) for ref in (east, flow, press)]
    for step in range(SUB):
        border(step, state[1], turn)
        border(SUB + step, work[2], 1.0)
        substep(state, work, inner, inner, inner, rate)
        state = work
    copies = []
    for field, ready, out in (
        (flow, ready_flow, flow_out),
        (east, ready_east, east_out),
    ):
        for rows in (0, 8):
            turn_out(field, rows, ready, by_row)
            some = pl.ds(rows, 8)
            copies.append(
                pltpu.make_async_copy(
                    ready.at[:, some], out.at[:, some], sems.at[len(copies)]
                )
            )
            copies[-1].start()
    for rows in (0, 8):
        turn_out(press, rows, press_out, by_row, 1.0 / half[...])
    for copy in copies:
        copy.wait()


def spread_kernel(press, heat_own, heat_back, out, ready, sems):
    even_lane = lane_iota() % 2 == 0
    even_row = sub_iota() % 2 == 0
    blocks = heat_own.shape[-1] // LANES
    copies = []
    for level in range(8):
        for block in range(2 * blocks):
            part = heat_own if block < blocks else heat_back
            value = part[level, :, pl.ds(block % blocks * LANES, LANES)]
            left = jnp.where(even_lane, value, pltpu.roll(value, 1, 1))
            right = jnp.where(even_lane, pltpu.roll(value, LANES - 1, 1), value)
            for side, heat in enumerate((left, right)):
                cols = pl.ds((2 * block + side) * LANES, LANES)
                top = jnp.where(even_row, heat, pltpu.roll(heat, 1, 0))
                bottom = jnp.where(even_row, pltpu.roll(heat, 7, 0), heat)
                ready[level, 0:8, cols] = press[level, 0:8, cols] + top
                ready[level, 8:16, cols] = press[level, 8:16, cols] + bottom
        copies.append(
            pltpu.make_async_copy(ready.at[level], out.at[level], sems.at[level])
        )
        copies[-1].start()
    for copy in copies:
        copy.wait()


def call(kernel, ins, outs, scratch=(), sems=None, more=(), limit=16):
    return pl.pallas_call(
        kernel,
        out_shape=[jax.ShapeDtypeStruct(shape, F32) for shape, _ in outs],
        in_specs=[pl.BlockSpec(memory_space=space) for space in ins],
        out_specs=[pl.BlockSpec(memory_space=space) for _, space in outs],
        scratch_shapes=[VMEM(shape, F32) for shape in scratch]
        + ([pltpu.SemaphoreType.DMA(sems)] if sems else [])
        + list(more),
        compiler_params=pltpu.CompilerParams(vmem_limit_bytes=limit << 20),
        cost_estimate=pl.CostEstimate(
            flops=10**7, bytes_accessed=10**7, transcendentals=0
        ),
    )


def shards(
    east_wind, equator_wind, pressure, moisture, albedo, courant, sun_angles, absorption, solar_weights
):
    east, flow, press, moist = east_wind[0], equator_wind[0], pressure[0], moisture[0]
    levels, rows, cols = east.shape
    n_tiles = lax.axis_size("tile")
    half_cols = cols // 4
    swap = [(0, 1), (1, 0)]

    def both_ways(pairs):
        return [pair for a, b in pairs for pair in ((a, b), (b, a))]

    mates = both_ways((t, t + 1) for t in range(0, n_tiles, 2))
    fars = both_ways(
        [
            (g * n_tiles + t, g * n_tiles + t + 1)
            for g in range(2)
            for t in range(1, n_tiles - 1, 2)
        ]
        + [(n_tiles - 1, 2 * n_tiles - 1)]
    )

    field = (levels, rows, cols)
    coarse = (9, 8, half_cols)
    staged = (rows, LANES, LANES)
    series = (2 * SUB, LANES, LANES)
    heat = (8, 8, half_cols)

    keep, send, east, flow, press, half, sun, absorb, weights = call(
        prepare_kernel,
        [HBM] * 9,
        [(coarse, VMEM)] * 2
        + [(staged, VMEM)] * 3
        + [((8, LANES), VMEM), ((2, 8, LANES), VMEM)]
        + [(absorption.shape, VMEM)] * 2,
        [field, albedo.shape[1:], field, field, field],
        (6, 4),
        [SMEM(courant.shape, F32), SMEM(sun_angles.shape, F32)],
    )(
        *(
            pltpu.with_memory_space_constraint(x, HBM)
            for x in (
                courant,
                sun_angles,
                absorption,
                solar_weights,
                moist,
                albedo[0],
                east,
                flow,
                press,
            )
        )
    )
    other = lax.ppermute(send, "group", swap)

    def alone(is_far):
        return call(
            functools.partial(alone_kernel, is_far),
            [VMEM] * 4,
            [(series, VMEM)] * 2,
            [(rows + 2 * OFF, LANES, LANES)] * 3,
        )(half, east, flow, press)

    own_far, far = alone(True)
    from_far = lax.ppermute(far, ("group", "tile"), fars)
    own_mate, mate = alone(False)
    from_mate = lax.ppermute(mate, "tile", mates)

    heat_own, heat_other = call(
        functools.partial(radiate_kernel, n_tiles * rows // 2, cols // 2),
        [SMEM] * 2 + [VMEM] * 3,
        [(heat, VMEM)] * 2,
    )(absorb, weights, sun, keep, other)
    heat_back = lax.ppermute(heat_other, "group", swap)

    east, flow, press = call(
        functools.partial(joined_kernel, n_tiles),
        [VMEM] * 8,
        [(field, HBM)] * 2 + [(field, VMEM)],
        [staged] * 3 + [(rows, 8, cols)] + [field] * 2,
        (4,),
    )(half, east, flow, press, own_mate, own_far, from_mate, from_far)
    (press,) = call(
        spread_kernel, [VMEM] * 3, [(field, HBM)], [field], (8,)
    )(press, heat_own, heat_back)
    return east[None], flow[None], press[None]


def solution(mesh):
    field = P("group", None, "tile", None)
    return jax.shard_map(
        shards,
        mesh=mesh,
        in_specs=(field,) * 4 + (P("group", "tile", None),) + (P(),) * 4,
        out_specs=(field,) * 3,
        check_vma=False,
    )
```

```python
import functools
import math

import jax
import jax.numpy as jnp
from jax import lax
from jax.experimental import pallas as pl
from jax.experimental.pallas import tpu as pltpu
from jax.sharding import PartitionSpec as P


SUB = 6
HEAT_SCALE = 10.0
MU_OFFSET = 0.1
DIFFUSE = 1.66
LOG2E = 1.4426950408889634
LANES = 128
OFF = 8

VMEM = pltpu.VMEM
SMEM = pltpu.SMEM
HBM = pltpu.HBM
F32 = jnp.float32


def lane_iota(dtype=jnp.int32):
    return lax.broadcasted_iota(dtype, (8, LANES), 1)


def sub_iota():
    return lax.broadcasted_iota(jnp.int32, (8, LANES), 0)


def coarsen(moist, albedo, keep, send):
    width = moist.shape[-1]
    half = keep.shape[-1] // LANES
    even_row = sub_iota() % 2 == 0
    even_lane = lane_iota() % 2 == 0

    def fold(top, bottom):
        return jnp.where(
            even_row, top + pltpu.roll(top, 7, 0), bottom + pltpu.roll(bottom, 1, 0)
        )

    def pack(left, right):
        return jnp.where(
            even_lane,
            left + pltpu.roll(left, LANES - 1, 1),
            right + pltpu.roll(right, 1, 1),
        )

    for level in range(9):
        for block in range(width // (2 * LANES)):
            parts = []
            for side in range(2):
                cols = pl.ds((2 * block + side) * LANES, LANES)
                source = moist if level < 8 else albedo
                index = (level,) if level < 8 else ()
                parts.append((source[(*index, slice(0, 8), cols)], source[(*index, slice(8, 16), cols)]))
            top = pack(parts[0][0], parts[1][0])
            bottom = pack(parts[0][1], parts[1][1])
            value = fold(top, bottom) * 0.25
            if block < half:
                keep[level, :, pl.ds(block * LANES, LANES)] = value
            else:
                send[level, :, pl.ds((block - half) * LANES, LANES)] = value


def turn_in(source, rows, target, scale=None):
    by_row = jnp.swapaxes(source[:, pl.ds(rows, 8), :], 0, 1)
    for row in range(8):
        blocks = [by_row[row][:, b * LANES : (b + 1) * LANES] for b in range(16)]
        flat = jnp.concatenate(blocks, axis=0).T
        values = []
        for half in range(2):
            eights = [flat[8 * k : 8 * k + 8] for k in range(half, 16, 2)]
            turned = jnp.swapaxes(jnp.stack(eights), 0, 1)
            values += [turned[i] for i in range(8)]
        if scale is not None:
            values = [scale * v for v in values]
        store_row(target, rows + row, values)


def turn_out(source, rows, target, by_row, scale=None):
    for row in range(rows, rows + 8):
        values = load_row(source, row)
        if scale is not None:
            values = [scale * v for v in values]
        halves = [jnp.swapaxes(jnp.stack(values[h : h + 8]), 0, 1) for h in (0, 8)]
        flat = jnp.concatenate([halves[k % 2][k // 2] for k in range(16)], axis=0)
        blocks = flat.T
        for b in range(16):
            by_row[row, :, pl.ds(b * LANES, LANES)] = blocks[8 * b : 8 * b + 8]
    target[:, pl.ds(rows, 8), :] = jnp.swapaxes(by_row[pl.ds(rows, 8)], 0, 1)


def prepare_kernel(
    courant_in,
    sun_in,
    absorption_in,
    weights_in,
    moist_in,
    albedo_in,
    east_in,
    flow_in,
    press_in,
    keep,
    send,
    east_0,
    flow_0,
    press_0,
    half_out,
    sun_out,
    absorption,
    weights,
    moist,
    albedo,
    east,
    flow,
    press,
    sems,
    courant,
    sun,
):
    fields = [(flow_in, flow), (east_in, east), (press_in, press)]
    copies = {
        ("small", 0): pltpu.make_async_copy(courant_in, courant, sems.at[0, 0]),
        ("small", 1): pltpu.make_async_copy(sun_in, sun, sems.at[0, 2]),
    }
    for n, (source, target) in enumerate(fields):
        for part in range(4):
            some = (pl.ds(part % 2 * 4, 4), pl.ds(part // 2 * 8, 8))
            copies[n, part // 2, part % 2] = pltpu.make_async_copy(
                source.at[some], target.at[some], sems.at[n + 1, part]
            )
    for part in range(4):
        some = pl.ds(2 * part, 2)
        copies["coarse", part] = pltpu.make_async_copy(
            moist_in.at[some], moist.at[some], sems.at[4, part]
        )
    copies["coarse", 4] = pltpu.make_async_copy(albedo_in, albedo, sems.at[0, 1])
    copies["rates", 0] = pltpu.make_async_copy(absorption_in, absorption, sems.at[0, 3])
    copies["rates", 1] = pltpu.make_async_copy(weights_in, weights, sems.at[5, 0])
    for copy in copies.values():
        copy.start()

    def wait(*key):
        for name, copy in copies.items():
            if name[: len(key)] == key:
                copy.wait()

    wait("small")
    half = courant_half(courant)
    half_out[...] = half
    for index in range(2):
        sun_out[index] = jnp.full((8, LANES), sun[index], F32)
    for n, (field, target, scale) in enumerate(
        ((flow, flow_0, None), (east, east_0, None), (press, press_0, half))
    ):
        for part in range(2):
            wait(n, part)
            turn_in(field, 8 * part, target, scale)
    wait("coarse")
    coarsen(moist, albedo, keep, send)
    wait("rates")


def radiate_kernel(
    rows_total, cols_total, first, absorption, weights, sun, own, other, heat_own, heat_other
):
    group = lax.axis_index("group")
    tile = lax.axis_index("tile")
    sublane = sub_iota()
    lane = lane_iota()
    row = tile * 8 + sublane // 2 + 4 * (sublane % 2)
    colatitude = 1.0 - (row.astype(F32) + 0.5) / rows_total
    hemisphere = 2.0 * group.astype(F32) - 1.0
    latitude = hemisphere * (0.5 * math.pi) * colatitude
    declination = 0.41 * jnp.sin(sun[0])
    sine = jnp.sin(latitude) * jnp.sin(declination)
    cosine = jnp.cos(latitude) * jnp.cos(declination)
    n_g = absorption.shape[0]

    for place in range(heat_own.shape[-1] // LANES):
        block = first + place
        cols = pl.ds(block * LANES, LANES)
        out_cols = pl.ds(place * LANES, LANES)
        column = block * LANES + lane // 2 + 64 * (lane % 2)
        longitude = 2.0 * math.pi * (column.astype(F32) + 0.5) / cols_total
        mu = sine + cosine * jnp.cos(longitude - sun[1])
        lit = mu > 0.0
        sunlit = jnp.abs(mu)
        slant = 1.0 / (sunlit + MU_OFFSET)
        depth = [jnp.zeros((8, LANES), F32)]
        for level in range(8):
            layer = jnp.where(lit, own[level, :, cols], other[level, :, cols])
            depth.append(depth[-1] + layer)
        surface = jnp.where(lit, own[8, :, cols], other[8, :, cols])
        total = depth[8]
        direct = total * slant
        paths = [depth[j] * slant for j in range(1, 9)]
        paths += [direct + DIFFUSE * (total - depth[j]) for j in range(8)]

        def body(g, carry):
            rate = absorption[g] * (-LOG2E)
            weight = weights[g]
            sums, whole = carry[:-1], carry[-1]
            sums = tuple(a + weight * jnp.exp2(rate * p) for a, p in zip(sums, paths))
            return sums + (whole + weight,)

        zero = jnp.zeros((8, LANES), F32)
        sums = lax.fori_loop(0, n_g, body, (zero,) * 17, unroll=32)
        down = (sums[16],) + sums[:8]
        up = sums[8:16] + (sums[7],)
        scale = sunlit * (HEAT_SCALE / n_g)
        net = [scale * (down[j] - surface * up[j]) for j in range(9)]
        for level in range(8):
            heat = net[level] - net[level + 1]
            heat_own[level, :, out_cols] = jnp.where(lit, heat, 0.0)
            heat_other[level, :, out_cols] = jnp.where(lit, 0.0, heat)


def courant_half(courant):
    level = lane_iota() % 8
    value = jnp.full((8, LANES), courant[7], F32)
    for index in range(7):
        value = jnp.where(level == index, courant[index], value)
    return 0.5 * value


def load_row(ref, row):
    return [ref[row, pl.ds(8 * i, 8), :] for i in range(16)]


def store_row(ref, row, values):
    for i, value in enumerate(values):
        if value is not None:
            ref[row, pl.ds(8 * i, 8), :] = value


def past_end(first):
    up = pltpu.roll(first, 7, 0)
    return jnp.where(sub_iota() == 7, pltpu.roll(up, LANES - 8, 1), up)


def before_start(last):
    down = pltpu.roll(last, 1, 0)
    return jnp.where(sub_iota() == 0, pltpu.roll(down, 8, 1), down)


def plus(values, others, sign=1.0):
    if others is None:
        return values
    if values is None:
        return others if sign > 0 else [-o for o in others]
    if sign > 0:
        return [v + o for v, o in zip(values, others)]
    return [v - o for v, o in zip(values, others)]


class Rows:
    def __init__(self, ref, first, rows=()):
        self.ref, self.first, self.known = ref, first, dict.fromkeys(rows)

    def get(self, row):
        if row not in self.known:
            return None
        if self.known[row] is not None:
            return self.known[row]
        return load_row(self.ref, row - self.first)

    def put(self, row, values):
        store_row(self.ref, row - self.first, values)
        self.known[row] = None


def substep(old, new, press_rows, flow_rows, east_rows, rate):
    east, flow, press = old
    new_east, new_flow, new_press = new
    every = sorted(set(press_rows) | {r + 1 for r in flow_rows})
    waiting = []

    def ends():
        row, before, after, pressures, winds = waiting.pop(0)
        low, high = pressures[0] - before, after - pressures[1]
        if winds is not None:
            low, high = winds[0] - low, winds[1] - high
        else:
            low, high = -low, -high
        new_east.put(row, [low] + [None] * 14 + [high])

    for row in every:
        if row in press_rows:
            change = plus(flow.get(row + 1), flow.get(row - 1), -1.0)
            winds = east.get(row)
            if winds is not None:
                ahead = winds[1:] + [past_end(winds[0])]
                behind = [before_start(winds[15])] + winds[:-1]
                change = plus([a - b for a, b in zip(ahead, behind)], change)
            change = [rate * c for c in change]
            here = plus(press.get(row), change, -1.0)
            new_press.put(row, here)
            if row in east_rows:
                slope = [here[i + 1] - here[i - 1] for i in range(1, 15)]
                inside = plus(winds and winds[1:15], slope, -1.0)
                new_east.put(row, [None] + inside + [None])
                waiting.append(
                    (
                        row,
                        before_start(here[15]),
                        past_end(here[0]),
                        (here[1], here[14]),
                        winds and (winds[0], winds[15]),
                    )
                )
        if row - 1 in flow_rows:
            slope = plus(new_press.get(row), new_press.get(row - 2), -1.0)
            new_flow.put(row - 1, plus(flow.get(row - 1), slope, -1.0))
        if len(waiting) > 2:
            ends()
    while waiting:
        ends()


PRESS_SPANS = [(-1, 10), (-3, 8), (-5, 6), (-5, 4), (-3, 2), (-1, 0)]
EAST_SPANS = [(-1, 8), (-3, 6), (-5, 4), (-3, 2), (-1, 0), (0, -1)]
FLOW_SPANS = [(-2, 9), (-4, 7), (-6, 5), (-4, 3), (-2, 1), (0, -1)]


def alone_kernel(
    is_far, half, east_0, flow_0, press_0, own, send, east, flow, press
):
    even = lax.axis_index("tile") % 2 == 0
    rate = half[...] * half[...]

    def run(place):
        def span(pair):
            return sorted(place(row) for row in range(pair[0], pair[1] + 1))

        def record(slot, rows):
            zero = [jnp.zeros((8, LANES), F32)] * 16
            store_row(own, slot, rows.get(place(-1)) or zero)
            store_row(send, slot, rows.get(place(0)))

        state = [Rows(ref, 0, range(16)) for ref in (east_0, flow_0, press_0)]
        work = [Rows(ref, -OFF) for ref in (east, flow, press)]
        for step in range(SUB):
            record(step, state[1])
            spans = [s[step] for s in (PRESS_SPANS, FLOW_SPANS, EAST_SPANS)]
            substep(state, work, *map(span, spans), rate)
            state = work
            record(SUB + step, state[2])

    low = even if is_far else jnp.logical_not(even)
    pl.when(low)(lambda: run(lambda row: row))
    pl.when(jnp.logical_not(low))(lambda: run(lambda row: 15 - row))


def joined_kernel(
    n_tiles,
    half,
    east_0,
    flow_0,
    press_0,
    own_mate,
    own_far,
    from_mate,
    from_far,
    east_out,
    flow_out,
    press_out,
    east,
    flow,
    press,
    by_row,
    ready_east,
    ready_flow,
    sems,
):
    tile = lax.axis_index("tile")
    even = tile % 2 == 0
    rate = half[...] * half[...]
    inner = range(16)
    keep = jnp.where(tile == 0, 0.0, 1.0)
    turn = jnp.where(tile == n_tiles - 1, -1.0, 1.0)

    def border(slot, rows, sign):
        mate = plus(load_row(own_mate, slot), load_row(from_mate, slot))
        far = [
            keep * o + sign * f
            for o, f in zip(load_row(own_far, slot), load_row(from_far, slot))
        ]
        rows.known[-1] = [jnp.where(even, f, m) for m, f in zip(mate, far)]
        rows.known[16] = [jnp.where(even, m, f) for m, f in zip(mate, far)]

    state = [Rows(ref, 0, inner) for ref in (east_0, flow_0, press_0)]
    work = [Rows(ref, 0) for ref in (east, flow, press)]
    for step in range(SUB):
        border(step, state[1], turn)
        border(SUB + step, work[2], 1.0)
        substep(state, work, inner, inner, inner, rate)
        state = work
    copies = []
    for field, ready, out in (
        (flow, ready_flow, flow_out),
        (east, ready_east, east_out),
    ):
        for rows in (0, 8):
            turn_out(field, rows, ready, by_row)
            some = pl.ds(rows, 8)
            copies.append(
                pltpu.make_async_copy(
                    ready.at[:, some], out.at[:, some], sems.at[len(copies)]
                )
            )
            copies[-1].start()
    for rows in (0, 8):
        turn_out(press, rows, press_out, by_row, 1.0 / half[...])
    for copy in copies:
        copy.wait()


def spread_kernel(press, own_1, own_2, back_1, back_2, out, ready, sems):
    even_lane = lane_iota() % 2 == 0
    even_row = sub_iota() % 2 == 0
    places = [
        (part, place)
        for part in (own_1, own_2, back_1, back_2)
        for place in range(part.shape[-1] // LANES)
    ]
    copies = []
    for level in range(8):
        for block, (part, place) in enumerate(places):
            value = part[level, :, pl.ds(place * LANES, LANES)]
            left = jnp.where(even_lane, value, pltpu.roll(value, 1, 1))
            right = jnp.where(even_lane, pltpu.roll(value, LANES - 1, 1), value)
            for side, heat in enumerate((left, right)):
                cols = pl.ds((2 * block + side) * LANES, LANES)
                top = jnp.where(even_row, heat, pltpu.roll(heat, 1, 0))
                bottom = jnp.where(even_row, pltpu.roll(heat, 7, 0), heat)
                ready[level, 0:8, cols] = press[level, 0:8, cols] + top
                ready[level, 8:16, cols] = press[level, 8:16, cols] + bottom
        copies.append(
            pltpu.make_async_copy(ready.at[level], out.at[level], sems.at[level])
        )
        copies[-1].start()
    for copy in copies:
        copy.wait()


def call(kernel, ins, outs, scratch=(), sems=None, more=(), limit=16):
    return pl.pallas_call(
        kernel,
        out_shape=[jax.ShapeDtypeStruct(shape, F32) for shape, _ in outs],
        in_specs=[pl.BlockSpec(memory_space=space) for space in ins],
        out_specs=[pl.BlockSpec(memory_space=space) for _, space in outs],
        scratch_shapes=[VMEM(shape, F32) for shape in scratch]
        + ([pltpu.SemaphoreType.DMA(sems)] if sems else [])
        + list(more),
        compiler_params=pltpu.CompilerParams(vmem_limit_bytes=limit << 20),
        cost_estimate=pl.CostEstimate(
            flops=10**7, bytes_accessed=10**7, transcendentals=0
        ),
    )


def shards(
    east_wind, equator_wind, pressure, moisture, albedo, courant, sun_angles, absorption, solar_weights
):
    east, flow, press, moist = east_wind[0], equator_wind[0], pressure[0], moisture[0]
    levels, rows, cols = east.shape
    n_tiles = lax.axis_size("tile")
    half_cols = cols // 4
    swap = [(0, 1), (1, 0)]

    def both_ways(pairs):
        return [pair for a, b in pairs for pair in ((a, b), (b, a))]

    mates = both_ways((t, t + 1) for t in range(0, n_tiles, 2))
    fars = both_ways(
        [
            (g * n_tiles + t, g * n_tiles + t + 1)
            for g in range(2)
            for t in range(1, n_tiles - 1, 2)
        ]
        + [(n_tiles - 1, 2 * n_tiles - 1)]
    )

    field = (levels, rows, cols)
    coarse = (9, 8, half_cols)
    staged = (rows, LANES, LANES)
    series = (2 * SUB, LANES, LANES)

    keep, send, east, flow, press, half, sun, absorb, weights = call(
        prepare_kernel,
        [HBM] * 9,
        [(coarse, VMEM)] * 2
        + [(staged, VMEM)] * 3
        + [((8, LANES), VMEM), ((2, 8, LANES), VMEM)]
        + [(absorption.shape, VMEM)] * 2,
        [field, albedo.shape[1:], field, field, field],
        (6, 4),
        [SMEM(courant.shape, F32), SMEM(sun_angles.shape, F32)],
    )(
        *(
            pltpu.with_memory_space_constraint(x, HBM)
            for x in (
                courant,
                sun_angles,
                absorption,
                solar_weights,
                moist,
                albedo[0],
                east,
                flow,
                press,
            )
        )
    )
    other = lax.ppermute(send, "group", swap)

    def alone(is_far):
        return call(
            functools.partial(alone_kernel, is_far),
            [VMEM] * 4,
            [(series, VMEM)] * 2,
            [(rows + 2 * OFF, LANES, LANES)] * 3,
        )(half, east, flow, press)

    own_far, far = alone(True)
    from_far = lax.ppermute(far, ("group", "tile"), fars)
    own_mate, mate = alone(False)
    from_mate = lax.ppermute(mate, "tile", mates)

    def radiate(first, count):
        shape = (8, 8, count * LANES)
        return call(
            functools.partial(radiate_kernel, n_tiles * rows // 2, cols // 2, first),
            [SMEM] * 2 + [VMEM] * 3,
            [(shape, VMEM)] * 2,
        )(absorb, weights, sun, keep, other)

    early = half_cols // LANES - 1
    own_1, other_1 = radiate(0, early)
    back_1 = lax.ppermute(other_1, "group", swap)
    own_2, other_2 = radiate(early, 1)
    back_2 = lax.ppermute(other_2, "group", swap)

    east, flow, press = call(
        functools.partial(joined_kernel, n_tiles),
        [VMEM] * 8,
        [(field, HBM)] * 2 + [(field, VMEM)],
        [staged] * 3 + [(rows, 8, cols)] + [field] * 2,
        (4,),
    )(half, east, flow, press, own_mate, own_far, from_mate, from_far)
    (press,) = call(
        spread_kernel, [VMEM] * 5, [(field, HBM)], [field], (8,)
    )(press, own_1, own_2, back_1, back_2)
    return east[None], flow[None], press[None]


def solution(mesh):
    field = P("group", None, "tile", None)
    return jax.shard_map(
        shards,
        mesh=mesh,
        in_specs=(field,) * 4 + (P("group", "tile", None),) + (P(),) * 4,
        out_specs=(field,) * 3,
        check_vma=False,
    )
```
